128 devices in a mesh: graph: 32 (over x, y, core), mp: 4 (over z).
Axes of the slice: x: 4, y: 4, z: 4, core: 2. Of those that a mesh axis runs over, the one named last changes fastest.
Arguments:
- edge_feats: bfloat16 [262144, 512], P('graph', 'mp'), may hold values from -6 to 6
- edge_source: int32 [262144], P('graph'), may hold values from 0 to 65535, as said below
- edge_target: int32 [262144], P('graph'), may hold values from 0 to 65535, as said below
- edge_live: int32 [262144], P('graph'), may hold values from 0 to 1, as said below
- trip_partner: int32 [8, 262144], P(None, 'graph'), may hold values from 0 to 262143, as said below
- trip_mask: int32 [8, 262144], P(None, 'graph'), may hold values 0 or 1
- trip_basis: bfloat16 [262144, 128], P('graph'), may hold values from -6 to 6
- atom_feats: bfloat16 [65536, 512], P('graph', 'mp'), may hold values from -6 to 6
- w_msg: bfloat16 [512, 512], P(None, 'mp'), may hold values from -0.25 to 0.25
- w_down: bfloat16 [512, 64], replicated, may hold values from -0.25 to 0.25
- w_bil: bfloat16 [1024, 64], replicated, may hold values from -0.1875 to 0.1875
- w_up: bfloat16 [64, 512], P(None, 'mp'), may hold values from -0.75 to 0.75
- w_atom: bfloat16 [512, 512], P(None, 'mp'), may hold values from -0.25 to 0.25
- w_edge: bfloat16 [512, 512], P(None, 'mp'), may hold values from -0.25 to 0.25
Outputs:
- edge_out: bfloat16 [262144, 512], P('graph', 'mp')
- atom_out: bfloat16 [65536, 512], P('graph', 'mp')
The draws below stay inside these ranges and needn't reach their ends.
Inputs may be any that keep to these rules, and one draw needn't show every extreme that they name: `edge_target`: edge slots lie in blocks of 256: the slots of graph shard g for destination shard d are slots (g * 32 + d) * 256 onward; every source atom of shard g's slots lies in atoms g * 2048 to (g + 1) * 2048 - 1, every target atom of a block for d in shard d's atoms. `edge_source`: source atoms belong to the shard that holds the slot. `edge_live`: in each block of 256 slots the live slots come first, at least one; in every draw some destination shard gets all 256 slots live from every source shard. `trip_partner`: A partner edge is a slot of the same block of 256 slots as the edge.
All inputs are finite; a program needn't handle non-finite values. No bound on the sum of `trip_mask` on one device may be relied on, other than what follows from the above.
Results may differ from the reference program's by a relative error of at most 0.01.
Values may be sent and summed in bfloat16 or wider, within the bound.
A program may use at most 192 MiB of HBM per device.

```python
import jax
import jax.numpy as jnp
from jax import lax

D = 512
DT = 64
NB = 16
SLOTS = 8
CAP = 256
ATOM_DEV = 2048
E_DEV = 8192
EDGES = 262144
ATOMS = 65536
N_GRAPH = 32


def bucket_counts(key):
    base = jax.random.randint(jax.random.fold_in(key, 11), (N_GRAPH, N_GRAPH), 1, CAP // 2 + 1)
    scores = jax.random.randint(jax.random.fold_in(key, 12), (N_GRAPH,), 0, 1 << 20)
    scores = scores * N_GRAPH + jnp.arange(N_GRAPH, dtype=jnp.int32)
    order = jnp.argsort(scores, stable=True)
    ranks = jnp.zeros((N_GRAPH,), jnp.int32).at[order].set(jnp.arange(N_GRAPH, dtype=jnp.int32))
    hot_dest = ranks < 3
    return jnp.where(hot_dest[None, :], CAP, base)


def slot_layout():
    position = jnp.arange(EDGES, dtype=jnp.int32)
    owner = position // (N_GRAPH * CAP)
    dest = position // CAP % N_GRAPH
    within = position % CAP
    return (owner, dest, within)


def draw_edge_live(key, part):
    counts = bucket_counts(key)
    owner, dest, within = slot_layout()
    return (within < counts[owner, dest]).astype(jnp.int32)


def draw_edge_target(key, part):
    owner, dest, within = slot_layout()
    local = jax.random.randint(jax.random.fold_in(key, 21), (EDGES,), 0, ATOM_DEV)
    return dest * ATOM_DEV + local


def draw_edge_source(key, part):
    owner, dest, within = slot_layout()
    local = jax.random.randint(jax.random.fold_in(key, 31), (EDGES,), 0, ATOM_DEV)
    return owner * ATOM_DEV + local


def draw_trip_partner(key, part):
    block_start = jnp.arange(EDGES, dtype=jnp.int32) // CAP * CAP
    local = jax.random.randint(jax.random.fold_in(key, 41), (SLOTS, EDGES), 0, CAP)
    return block_start[None, :] + local


def place_ends(values, stream_key, low, high):
    spot = [jax.random.randint(jax.random.fold_in(stream_key, axis), (), 0, length) for axis, length in enumerate(values.shape)]
    widest = values.shape.index(max(values.shape))
    next_to = spot[:widest] + [(spot[widest] + 1) % values.shape[widest]] + spot[widest + 1:]
    return values.at[tuple(spot)].set(low).at[tuple(next_to)].set(high)


def steps_of(rng, shape, shards, smallest, largest):
    gain = 1.0
    for dim, shards_of in shards:
        heights = jax.random.uniform(jax.random.fold_in(jax.random.fold_in(rng, 6), dim), (shards_of,), jnp.float32, smallest / len(shards), largest / len(shards))
        gain = gain * jnp.repeat(jnp.exp(heights), shape[dim] // shards_of).reshape((-1,) + (1,) * (len(shape) - 1 - dim))
    return gain


def normal_values(key, dims, deviation, most, split=(), held_as=jnp.bfloat16):
    factor_of = steps_of(key, dims, split, -0.22, 0.18) if split else 1.0
    values = jax.random.normal(key, dims, jnp.float32) * deviation * factor_of
    return jnp.minimum(jnp.maximum(values, -most), most).astype(held_as)


def setup_inputs(seed: int = 0) -> dict:
    arg_keys = jax.random.split(jax.random.key(seed), 15)
    edge_feats = normal_values(arg_keys[0], (EDGES, D), 1.0, 6.0, ((0, 32), (1, 4)))
    edge_source = draw_edge_source(jax.random.fold_in(arg_keys[14], 71), 0)
    edge_target = draw_edge_target(jax.random.fold_in(arg_keys[14], 71), 0)
    edge_live = draw_edge_live(jax.random.fold_in(arg_keys[14], 71), 0)
    trip_partner = draw_trip_partner(jax.random.fold_in(arg_keys[14], 71), 0)
    trip_mask = place_ends((jax.random.randint(arg_keys[5], (SLOTS, EDGES), 0, 4) < 3).astype(jnp.int32), jax.random.fold_in(arg_keys[5], 1), 0, 1)
    trip_basis = normal_values(arg_keys[6], (EDGES, SLOTS * NB), 1.0, 6.0, ((0, 32),))
    atom_feats = normal_values(arg_keys[7], (ATOMS, D), 1.0, 6.0, ((0, 32), (1, 4)))
    w_msg = normal_values(arg_keys[8], (D, D), D ** -0.5, 0.25, ((1, 4),))
    w_down = normal_values(arg_keys[9], (D, DT), D ** -0.5, 0.25)
    w_bil = normal_values(arg_keys[10], (NB * DT, DT), (NB * DT) ** -0.5, 0.1875)
    w_up = normal_values(arg_keys[11], (DT, D), DT ** -0.5, 0.75, ((1, 4),))
    w_atom = normal_values(arg_keys[12], (D, D), D ** -0.5, 0.25, ((1, 4),))
    w_edge = normal_values(arg_keys[13], (D, D), D ** -0.5, 0.25, ((1, 4),))
    return {"edge_feats": edge_feats, "edge_source": edge_source, "edge_target": edge_target, "edge_live": edge_live, "trip_partner": trip_partner, "trip_mask": trip_mask, "trip_basis": trip_basis, "atom_feats": atom_feats, "w_msg": w_msg, "w_down": w_down, "w_bil": w_bil, "w_up": w_up, "w_atom": w_atom, "w_edge": w_edge}


def reference(edge_feats, edge_source, edge_target, edge_live, trip_partner, trip_mask, trip_basis, atom_feats, w_msg, w_down, w_bil, w_up, w_atom, w_edge):
    hid = jnp.dot(edge_feats, w_msg, preferred_element_type=jnp.float32)
    message = edge_feats.astype(jnp.float32) + jax.nn.silu(hid)
    down = jnp.dot(edge_feats, w_down, preferred_element_type=jnp.float32).astype(jnp.bfloat16)
    blocks = EDGES // E_DEV

    def one_block(index):
        begin = (index * E_DEV).astype(jnp.int32)
        partner = lax.dynamic_slice_in_dim(trip_partner, begin, E_DEV, 1)
        masked = lax.dynamic_slice_in_dim(trip_mask, begin, E_DEV, 1)
        basis = lax.dynamic_slice_in_dim(trip_basis, begin, E_DEV, 0).reshape(E_DEV, SLOTS, NB)
        weights = basis.astype(jnp.float32) * jnp.transpose(masked).astype(jnp.float32)[:, :, None]
        picked = jnp.take(down, partner, axis=0).astype(jnp.float32)
        mixed = jnp.einsum('esb,sea->eba', weights, picked).astype(jnp.bfloat16)
        return jnp.dot(mixed.reshape(E_DEV, NB * DT), w_bil, preferred_element_type=jnp.float32).astype(jnp.bfloat16)

    bil = lax.map(one_block, jnp.arange(blocks, dtype=jnp.int32)).reshape(EDGES, DT)
    total = message + jnp.dot(bil, w_up, preferred_element_type=jnp.float32)
    outgoing = (total * edge_live.astype(jnp.float32)[:, None]).astype(jnp.bfloat16)
    agg = jax.ops.segment_sum(outgoing.astype(jnp.float32), edge_target, num_segments=ATOMS)
    atom_mid = (atom_feats.astype(jnp.float32) + agg).astype(jnp.bfloat16)
    ahid = jnp.dot(atom_mid, w_atom, preferred_element_type=jnp.float32)
    atom_out = (atom_mid.astype(jnp.float32) + jax.nn.silu(ahid)).astype(jnp.bfloat16)
    pair = (jnp.take(atom_out, edge_source, axis=0).astype(jnp.float32) * jnp.take(atom_out, edge_target, axis=0).astype(jnp.float32)).astype(jnp.bfloat16)
    ehid = jnp.dot(pair, w_edge, preferred_element_type=jnp.float32)
    edge_out = (total + jax.nn.silu(ehid)).astype(jnp.bfloat16)
    return edge_out, atom_out
```

```python
import jax
import jax.numpy as jnp
from jax import lax
from jax.experimental import pallas as pl
from jax.experimental.pallas import tpu as pltpu
from jax.sharding import PartitionSpec as P

DT = 64
NB = 16
SLOTS = 8
CAP = 256
MP = 4
BF = jnp.bfloat16
F32 = jnp.float32


def triplet_kernel(down_ref, ids_ref, basis_ref, rep_ref, tile_ref, wbil_ref, out_ref):
    nblk = down_ref.shape[0]
    q = ids_ref.shape[0] // nblk
    weights = jnp.dot(basis_ref[...], tile_ref[...], preferred_element_type=F32)
    lanes = lax.broadcasted_iota(jnp.int32, (q, CAP), 1)
    for k in range(nblk):
        rows = slice(k * q, (k + 1) * q)
        table = jnp.dot(down_ref[k], rep_ref[...], preferred_element_type=F32).astype(BF)
        ids = ids_ref[rows, :]
        onehot = jnp.concatenate(
            [(ids[:, s : s + 1] == lanes).astype(F32).astype(BF) for s in range(SLOTS)], axis=0
        )
        bil = jnp.zeros((q, DT), F32)
        for j in range(4):
            cols = slice(256 * j, 256 * (j + 1))
            picked = jnp.dot(onehot, table[:, cols], preferred_element_type=F32)
            mixed = jnp.zeros((q, 256), F32)
            for s in range(SLOTS):
                w = weights[rows, 128 * s : 128 * (s + 1)]
                mixed = mixed + picked[s * q : (s + 1) * q] * jnp.concatenate([w, w], axis=1)
            bil = bil + jnp.dot(mixed.astype(BF), wbil_ref[cols, :], preferred_element_type=F32)
        out_ref[rows, :] = bil.astype(BF)


def triplets(down_all, ids, basis, w_bil):
    nblk = down_all.shape[0]
    rows = ids.shape[0]
    q = rows // nblk
    step = 4
    a = jnp.arange(NB * DT, dtype=jnp.int32)
    rep = (a[None, :] // NB == jnp.arange(DT, dtype=jnp.int32)[:, None]).astype(BF)
    src = (a // 128) * NB + a % NB
    tile = (src[None, :] == jnp.arange(128, dtype=jnp.int32)[:, None]).astype(BF)
    wperm = jnp.transpose(w_bil.reshape(NB, DT, DT), (1, 0, 2)).reshape(NB * DT, DT)
    return pl.pallas_call(
        triplet_kernel,
        grid=(nblk // step,),
        in_specs=[
            pl.BlockSpec((step, CAP, DT), lambda i: (i, 0, 0)),
            pl.BlockSpec((step * q, SLOTS), lambda i: (i, 0)),
            pl.BlockSpec((step * q, 128), lambda i: (i, 0)),
            pl.BlockSpec((DT, NB * DT), lambda i: (0, 0)),
            pl.BlockSpec((128, NB * DT), lambda i: (0, 0)),
            pl.BlockSpec((NB * DT, DT), lambda i: (0, 0)),
        ],
        out_specs=pl.BlockSpec((step * q, DT), lambda i: (i, 0)),
        out_shape=jax.ShapeDtypeStruct((rows, DT), BF),
        name="triplets",
    )(down_all, ids, basis, rep, tile, wperm)


def local(
    edge_feats,
    edge_source,
    edge_target,
    edge_live,
    trip_partner,
    trip_mask,
    trip_basis,
    atom_feats,
    w_msg,
    w_down,
    w_bil,
    w_up,
    w_atom,
    w_edge,
):
    n_edges = edge_feats.shape[0]
    width = edge_feats.shape[1]
    full = width * MP
    atoms_local = atom_feats.shape[0]
    blocks = n_edges // CAP
    q = CAP // MP
    rows = blocks * q
    m = lax.axis_index("mp")

    def quarter(v):
        return lax.dynamic_index_in_dim(
            v.reshape((blocks, MP, q) + v.shape[1:]), m, axis=1, keepdims=False
        )

    def gather_w(w):
        return lax.all_gather(w, "mp", axis=1, tiled=True)

    target_q = quarter(edge_target) % atoms_local
    source_q = (quarter(edge_source) % atoms_local).reshape(rows)
    live_q = quarter(edge_live).reshape(rows)
    in_ids = lax.all_to_all(target_q, "graph", split_axis=0, concat_axis=0, tiled=True).reshape(rows)

    pm = jnp.where(trip_mask != 0, trip_partner % CAP, -1)
    pm = lax.dynamic_index_in_dim(
        pm.reshape(SLOTS, blocks, MP, q), m, axis=2, keepdims=False
    ).reshape(SLOTS, rows)
    ids = jnp.transpose(pm)
    basis = quarter(trip_basis).reshape(rows, 128)

    x = lax.all_to_all(
        edge_feats.reshape(blocks, MP, q, width), "mp", split_axis=1, concat_axis=1, tiled=True
    )
    x = jnp.transpose(x, (0, 2, 1, 3)).reshape(rows, full)
    w_msg_f = gather_w(w_msg)
    w_up_f = gather_w(w_up)
    down = jnp.dot(x, w_down, preferred_element_type=F32).astype(BF)
    down_all = lax.all_gather(down.reshape(blocks, q, DT), "mp", axis=1, tiled=True)
    hid = jnp.dot(x, w_msg_f, preferred_element_type=F32)
    message = x.astype(F32) + jax.nn.silu(hid)
    bil = triplets(down_all, ids, basis, w_bil)
    total = message + jnp.dot(bil, w_up_f, preferred_element_type=F32)
    outgoing = (total * live_q.astype(F32)[:, None]).astype(BF)
    incoming = lax.all_to_all(
        outgoing.reshape(blocks, q, full), "graph", split_axis=0, concat_axis=0, tiled=True
    ).reshape(rows, full)
    atom_ids = jnp.arange(atoms_local, dtype=jnp.int32)
    onehot_in = (atom_ids[:, None] == in_ids[None, :]).astype(BF)
    partial = jnp.dot(onehot_in, incoming, preferred_element_type=F32).astype(BF)
    quarter_atoms = atoms_local // MP
    parts = lax.all_to_all(
        partial.reshape(MP, quarter_atoms, full), "mp", split_axis=0, concat_axis=0, tiled=True
    )
    arow = lax.all_to_all(
        atom_feats.reshape(MP, quarter_atoms, width), "mp", split_axis=0, concat_axis=0, tiled=True
    )
    arow = jnp.transpose(arow, (1, 0, 2)).reshape(quarter_atoms, full)
    atom_mid = (arow.astype(F32) + jnp.sum(parts.astype(F32), axis=0)).astype(BF)
    ahid = jnp.dot(atom_mid, gather_w(w_atom), preferred_element_type=F32)
    atom_rows = (atom_mid.astype(F32) + jax.nn.silu(ahid)).astype(BF)
    atom_full = lax.all_gather(atom_rows, "mp", axis=0, tiled=True)
    atom_out = lax.dynamic_slice_in_dim(atom_full, m * width, width, axis=1)

    onehot_t = (in_ids[:, None] == atom_ids[None, :]).astype(BF)
    target_rows = jnp.dot(onehot_t, atom_full, preferred_element_type=F32).astype(BF)
    target_rows = lax.all_to_all(
        target_rows.reshape(blocks, q, full), "graph", split_axis=0, concat_axis=0, tiled=True
    ).reshape(rows, full)
    onehot_s = (source_q[:, None] == atom_ids[None, :]).astype(BF)
    source_rows = jnp.dot(onehot_s, atom_full, preferred_element_type=F32)
    pair = (source_rows * target_rows.astype(F32)).astype(BF)
    ehid = jnp.dot(pair, gather_w(w_edge), preferred_element_type=F32)
    edge_rows = (total + jax.nn.silu(ehid)).astype(BF)
    back = jnp.transpose(edge_rows.reshape(blocks, q, MP, width), (0, 2, 1, 3))
    edge_out = lax.all_to_all(back, "mp", split_axis=1, concat_axis=1, tiled=True)
    return (edge_out.reshape(n_edges, width), atom_out)


def solution(mesh):
    return jax.shard_map(
        local,
        mesh=mesh,
        in_specs=(
            P("graph", "mp"),
            P("graph"),
            P("graph"),
            P("graph"),
            P(None, "graph"),
            P(None, "graph"),
            P("graph", None),
            P("graph", "mp"),
            P(None, "mp"),
            P(),
            P(),
            P(None, "mp"),
            P(None, "mp"),
            P(None, "mp"),
        ),
        out_specs=(P("graph", "mp"), P("graph", "mp")),
        check_vma=False,
    )
```

```python
import jax
import jax.numpy as jnp
from jax import lax
from jax.experimental import pallas as pl
from jax.experimental.pallas import tpu as pltpu
from jax.sharding import PartitionSpec as P

DT = 64
NB = 16
SLOTS = 8
CAP = 256
MP = 4
Q = CAP // MP
NG = 32
BLK = 8
D = 512
W = D // MP
ORDER = (2, 1, 3, 0)
BF = jnp.bfloat16
F32 = jnp.float32
MESH = pl.DeviceIdType.MESH


def silu(v):
    h = 0.5 * v
    return h + h * jnp.tanh(h)


def dot(a, b):
    return jnp.dot(a, b, preferred_element_type=F32)


def lanes_at(k, n):
    return pl.ds(pl.multiple_of(k * n, n), n)


def rows_at(k, n):
    return pl.ds(pl.multiple_of(k * n, n), n)


def enter(g, m, over_graph):
    sem = pltpu.get_barrier_semaphore()
    peers = [(g, (m + k) % MP) for k in range(1, MP)]
    if over_graph:
        peers += [((g + k) % NG, m) for k in range(1, NG)]
    for peer in peers:
        pl.semaphore_signal(sem, inc=1, device_id=peer, device_id_type=MESH)
    pl.semaphore_wait(sem, len(peers))


def remote(src, dst, send, recv, peer):
    return pltpu.make_async_remote_copy(
        src_ref=src, dst_ref=dst, send_sem=send, recv_sem=recv, device_id=peer, device_id_type=MESH
    )


def low_lanes(shape):
    return lax.broadcasted_iota(jnp.int32, shape, len(shape) - 1) < Q


def pair_row(ref, blk, m):
    half = m // 2
    a = ref[pl.ds(2 * blk + half, 1), :]
    b = ref[pl.ds(2 * blk + 2 + half, 1), :]
    odd = m % 2 == 1
    ra, rb = pltpu.roll(a, Q, 1), pltpu.roll(b, Q, 1)
    return jnp.where(low_lanes(a.shape), jnp.where(odd, ra, a), jnp.where(odd, b, rb))


def column(row):
    return jnp.transpose(jnp.broadcast_to(row.astype(F32), (128, 128)))


def message_kernel(
    ef,
    target,
    live,
    partner,
    mask,
    basis,
    w_msg,
    w_down,
    l_mat,
    w_up,
    w_atom,
    w_edge,
    af,
    total,
    incoming,
    in_ids,
    atom_f,
    edge_f,
    arow,
    x,
    dall,
    at,
    wrow,
    outg,
    idq,
    msg_f,
    up_f,
    zs,
    zr,
    zl,
    xs,
    xr,
    xl,
):
    g = lax.axis_index("graph")
    m = lax.axis_index("mp")
    enter(g, m, True)
    quarter_atoms = arow.shape[0]
    own = lanes_at(m, W)

    def group(c):
        return (g // BLK + c) % 4

    def blocks_of(c):
        return pl.ds(pl.multiple_of(group(c) * BLK, BLK), BLK)

    def exchange(kind, src_of, dst):
        for j in (2, 1, 3):
            t = (m + j) % MP
            remote(src_of(t), dst, zs.at[kind, j], zr.at[kind, j], (g, t)).start()

    def local(kind, src, dst):
        pltpu.make_async_copy(src, dst, zl.at[kind]).start()

    def moves(kind):
        if kind < 4:
            b = blocks_of(ORDER[kind])
            return (lambda t: ef.at[b, t]), x.at[b, :, own], ef.at[b, m]
        if kind < 8:
            p = pl.ds(pl.multiple_of(group(ORDER[kind - 4]) * 4, 4), 4)
            d = dall.at[p, rows_at(m, Q), :]
            return (lambda t: d), d, None
        if kind == 12:
            return (
                (lambda t: af.at[t]),
                arow.at[:, own],
                af.at[m],
            )
        src, dst = ((w_msg, msg_f), (w_up, up_f), (w_atom, atom_f), (w_edge, edge_f))[kind - 8]
        return (lambda t: src), dst.at[:, own], src

    def start(kind):
        src_of, dst, here = moves(kind)
        if here is not None:
            local(kind, here, dst)
        exchange(kind, src_of, dst)

    def arrived(kind):
        src_of, dst, here = moves(kind)
        if here is not None:
            pltpu.make_async_copy(here, dst, zl.at[kind]).wait()
        for j in (2, 1, 3):
            t = (m + j) % MP
            remote(src_of(t), dst, zs.at[kind, j], zr.at[kind, j], (g, t)).wait_recv()

    def sent(kind):
        src_of, dst, here = moves(kind)
        for j in (2, 1, 3):
            t = (m + j) % MP
            remote(src_of(t), dst, zs.at[kind, j], zr.at[kind, j], (g, t)).wait_send()

    start(0)
    start(8)
    start(9)
    start(1)

    def write_ids(p, carry):
        row = pair_row(target, 2 * p, m) & 2047
        idq[2 * p] = row
        idq[2 * p + 1] = pltpu.roll(row, Q, 1)
        return carry

    lax.fori_loop(0, NG // 2, write_ids, 0)

    def weights_of(blk0):
        t = jnp.transpose(
            jnp.concatenate([basis[blk0, m], basis[blk0 + 1, m]], axis=0).astype(F32)
        ).reshape(SLOTS, 2, 8, 128)
        lo, hi = t[:, 0], t[:, 1]
        low = low_lanes((SLOTS, 8, 128))
        return (
            jnp.where(low, lo, pltpu.roll(hi.reshape(64, 128), Q, 1).reshape(SLOTS, 8, 128)),
            jnp.where(low, pltpu.roll(lo.reshape(64, 128), Q, 1).reshape(SLOTS, 8, 128), hi),
        )

    def ids_of(blk):
        cols = lanes_at(2 * blk + m // 2, 128)
        v = jnp.where(mask[:, cols] != 0, partner[:, cols] & 255, -1)
        r = pltpu.roll(v, Q, 1)
        odd = m % 2 == 1
        low = low_lanes(v.shape)
        return jnp.where(low, jnp.where(odd, r, v), jnp.where(odd, v, r))

    def spread_pair(c, i):
        blk0 = group(c) * BLK + 2 * i
        both = weights_of(blk0)
        for half in range(2):
            blk = blk0 + half
            w = both[half]
            for s in range(SLOTS):
                for j in range(8):
                    wrow[s * 8 + j] = jnp.broadcast_to(w[s, j : j + 1, :], (16, 128)).astype(BF)
            ids = ids_of(blk)

            def part(pt, carry):
                p_ids = lax.broadcasted_iota(jnp.int32, (32, 128), 0) + 32 * pt
                acc = [jnp.zeros((2, 16, 128), BF) for _ in range(8)]
                for s in range(SLOTS):
                    hot = (
                        jnp.where(ids[s : s + 1, :] == p_ids, 1.0, 0.0).astype(BF).reshape(2, 16, 128)
                    )
                    for j in range(8):
                        acc[j] = acc[j] + hot * wrow[s * 8 + j][None]
                for j in range(8):
                    at[blk, rows_at(pt, 32), 128 * j : 128 * (j + 1)] = acc[j].reshape(32, 128)
                return carry

            lax.fori_loop(0, 8, part, 0)

    def spread(c):
        def body(i, carry):
            spread_pair(c, i)
            return carry

        lax.fori_loop(0, BLK // 2, body, 0)

    def down(c):
        def body(i, carry):
            blk0 = group(c) * BLK + 2 * i
            rows = x[pl.ds(blk0, 2)].reshape(128, D)
            d = dot(rows, w_down[...])
            dall[group(c) * 4 + i, rows_at(m, Q), :] = jnp.concatenate(
                [d[:Q], d[Q:]], axis=1
            ).astype(BF)
            return carry

        lax.fori_loop(0, BLK // 2, body, 0)

    def hidden(c):
        def body(i, carry):
            blk0 = group(c) * BLK + 2 * i
            rows = x[pl.ds(blk0, 2)].reshape(128, D)
            total[rows_at(group(c) * 4 + i, 128), :] = rows.astype(F32) + silu(
                dot(rows, msg_f[...])
            )
            return carry

        lax.fori_loop(0, BLK // 2, body, 0)

    def finish(c):
        def body(i, carry):
            p = group(c) * 4 + i
            blk0 = 2 * p
            dt = jnp.transpose(dall[p].astype(F32)).astype(BF)
            sides = []
            for half in range(2):
                mixed = dot(dt[half * DT : (half + 1) * DT], at[blk0 + half]).astype(BF)
                sides.append(
                    jnp.concatenate([mixed[:, 128 * j : 128 * (j + 1)] for j in range(8)], axis=0)
                )
            o = dot(l_mat[...], jnp.concatenate(sides, axis=1))
            a, b = o[:, :128], o[:, 128:]
            low = low_lanes((DT, 128))
            bil_t = jnp.where(
                low, a[:DT] + pltpu.roll(a[DT:], Q, 1), pltpu.roll(b[:DT], Q, 1) + b[DT:]
            )
            bil = jnp.transpose(bil_t).astype(BF)
            rows = rows_at(p, 128)
            tot = total[rows, :] + dot(bil, up_f[...])
            total[rows, :] = tot
            alive = column(pair_row(live, blk0, m))
            alive = jnp.concatenate([alive] * 4, axis=1)
            outg[pl.ds(blk0, 2)] = (tot * alive).astype(BF).reshape(2, Q, D)
            return carry

        lax.fori_loop(0, BLK // 2, body, 0)

    def block_copy(n, d):
        return remote(outg.at[d], incoming.at[g], xs.at[0, n], xr.at[0, g], (d, m))

    def ids_copy(n, d):
        return remote(idq.at[d], in_ids.at[g], xs.at[1, n], xr.at[1, g], (d, m))

    def others(c):
        if c == 0:
            return [(24 + k, group(c) * BLK + (g + k) % BLK) for k in range(1, BLK)]
        return [(8 * ORDER.index(c) + k, group(c) * BLK + k) for k in range(BLK)]

    def send(c):
        if c == 0:
            pltpu.make_async_copy(outg.at[g], incoming.at[g], xl.at[0]).start()
            pltpu.make_async_copy(idq.at[g], in_ids.at[g], xl.at[1]).start()
        for n, d in others(c):
            block_copy(n, d).start()
            ids_copy(n, d).start()

    spread(ORDER[0])
    spread(ORDER[1])
    arrived(0)
    down(ORDER[0])
    start(4)
    start(2)
    arrived(8)
    hidden(ORDER[0])
    spread(ORDER[2])
    arrived(1)
    down(ORDER[1])
    start(5)
    start(3)
    arrived(9)
    arrived(4)
    finish(ORDER[0])
    hidden(ORDER[1])
    send(ORDER[0])
    spread(ORDER[3])
    arrived(2)
    down(ORDER[2])
    start(6)
    arrived(5)
    finish(ORDER[1])
    hidden(ORDER[2])
    send(ORDER[1])
    arrived(3)
    down(ORDER[3])
    start(7)
    start(12)
    start(10)
    start(11)
    arrived(6)
    finish(ORDER[2])
    hidden(ORDER[3])
    send(ORDER[2])
    arrived(7)
    finish(ORDER[3])
    send(ORDER[3])
    for kind in (10, 11, 12):
        arrived(kind)
    for kind in range(13):
        sent(kind)
    pltpu.make_async_copy(outg.at[g], incoming.at[g], xl.at[0]).wait()
    pltpu.make_async_copy(idq.at[g], in_ids.at[g], xl.at[1]).wait()
    for k in range(1, NG):
        s = (g + k) % NG
        remote(outg.at[s], incoming.at[s], xs.at[0, 0], xr.at[0, s], (s, m)).wait_recv()
        remote(idq.at[s], in_ids.at[s], xs.at[1, 0], xr.at[1, s], (s, m)).wait_recv()
    for c in ORDER:
        for n, d in others(c):
            block_copy(n, d).wait_send()
            ids_copy(n, d).wait_send()


def atom_kernel(inc, ids, arow, atom_f, afull, aout, idr, pbuf, rbuf, own, hot, ps, pr, us, ur):
    g = lax.axis_index("graph")
    m = lax.axis_index("mp")
    enter(g, m, False)
    quarter = arow.shape[0]
    h2 = quarter // 2
    up, dn = (m + 1) % MP, (m + 3) % MP

    def pairs(i, carry):
        a, b = ids[2 * i], ids[2 * i + 1]
        idr[pl.ds(i, 1), :] = jnp.where(low_lanes(a.shape), a, pltpu.roll(b, Q, 1))
        return carry

    lax.fori_loop(0, NG // 2, pairs, 0)

    def part(j, h):
        base = ((m + j) % MP) * quarter + h * h2

        def build(i, carry):
            at = lax.broadcasted_iota(jnp.int32, (h2, 128), 0) + base
            hot[:, lanes_at(i, 128)] = jnp.where(idr[pl.ds(i, 1), :] == at, 1.0, 0.0).astype(BF)
            return carry

        lax.fori_loop(0, NG // 2, build, 0)
        return dot(hot[...], inc[...])

    def copy(j, h):
        t = (m + j) % MP
        rows = pl.ds(h * h2, h2)
        return remote(pbuf.at[j, rows], rbuf.at[j, rows], ps.at[j, h], pr.at[j, h], (g, t))

    waiting = None
    for j in ORDER:
        for h in range(2):
            v = part(j, h)
            if j == 0:
                own[h * h2 : (h + 1) * h2, :] = v + arow[h * h2 : (h + 1) * h2, :].astype(F32)
            else:
                pbuf[j, h * h2 : (h + 1) * h2, :] = v.astype(BF)
            if waiting is not None:
                copy(*waiting).start()
                waiting = None
            if j != 0:
                waiting = (j, h)

    def rows_of(src, h):
        return afull.at[pl.ds(pl.multiple_of(src * quarter + h * h2, h2), h2)]

    def own_copy(h, to):
        t = up if to == 0 else dn
        return remote(rows_of(m, h), rows_of(m, h), us.at[to, h], ur.at[to, h], (g, t))

    def relay(to):
        src, t = (dn, up) if to == 0 else (up, dn)
        return remote(rows_of(src, to), rows_of(src, to), us.at[2, to], ur.at[2, to], (g, t))

    for h in range(2):
        rows = slice(h * h2, (h + 1) * h2)
        for j in (2, 1, 3):
            copy(j, h).wait_recv()
        s = own[rows, :]
        for j in (1, 2, 3):
            s = s + rbuf[j, rows, :].astype(F32)
        mid = s.astype(BF)
        out = (mid.astype(F32) + silu(dot(mid, atom_f[...]))).astype(BF)
        afull[pl.ds(pl.multiple_of(m * quarter + h * h2, h2), h2), :] = out
        for to in (h, 1 - h):
            own_copy(h, to).start()
    own_copy(0, 0).wait_recv()
    relay(0).start()
    own_copy(1, 1).wait_recv()
    relay(1).start()
    own_copy(0, 1).wait_recv()
    own_copy(1, 0).wait_recv()
    relay(0).wait_recv()
    relay(1).wait_recv()
    aout[...] = afull[:, lanes_at(m, W)]
    for h in range(2):
        for j in (1, 2, 3):
            copy(j, h).wait_send()
        for to in range(2):
            own_copy(h, to).wait_send()
        relay(h).wait_send()


def edge_kernel(afull, ids, source, total, edge_f, out, hot, sbuf, tbuf, src, ebuf, xs, xr, xl, zs, zr, zl):
    g = lax.axis_index("graph")
    m = lax.axis_index("mp")
    enter(g, m, True)
    n_atoms = afull.shape[0]

    def group(c):
        return (g // BLK + c) % 4

    def pick(row_of):
        def build(i, carry):
            col = column(row_of(i))
            for k in range(n_atoms // 128):
                lane = lax.broadcasted_iota(jnp.int32, (128, 128), 1).astype(F32) + 128.0 * k
                hot[rows_at(i, 128), 128 * k : 128 * (k + 1)] = jnp.where(
                    col == lane, 1.0, 0.0
                ).astype(BF)
            return carry

        lax.fori_loop(0, BLK // 2, build, 0)
        return dot(hot[...], afull[...]).astype(BF).reshape(BLK, Q, D)

    def others(c):
        if c == 0:
            return [(24 + k, group(c) * BLK + (g + k) % BLK) for k in range(1, BLK)]
        return [(8 * ORDER.index(c) + k, group(c) * BLK + k) for k in range(BLK)]

    def block_copy(n, d):
        return remote(sbuf.at[d], tbuf.at[g], xs.at[n], xr.at[g], (d, m))

    def send(c):
        if c == 0:
            pltpu.make_async_copy(sbuf.at[g], tbuf.at[g], xl).start()
        for n, d in others(c):
            block_copy(n, d).start()

    def blocks_at(gr):
        return pl.ds(pl.multiple_of(gr * BLK, BLK), BLK)

    previous = None
    for c in ORDER:

        def row_of(i, c=c):
            blk0 = group(c) * BLK + 2 * i
            a, b = ids[blk0], ids[blk0 + 1]
            return jnp.where(low_lanes(a.shape), a, pltpu.roll(b, Q, 1))

        sbuf[blocks_at(group(c))] = pick(row_of)
        if previous is not None:
            send(previous)
        previous = c
    for n, c in enumerate(ORDER):

        def row_of(i, c=c):
            blk0 = group(-c) * BLK + 2 * i
            return pair_row(source, blk0, m) & 2047

        src[blocks_at(group(-c))] = pick(row_of)
        if n == 0:
            send(previous)

    def back(c, j):
        b = blocks_at(group(-c))
        t = (m + j) % MP
        n = ORDER.index(c)
        return remote(
            ebuf.at[b, :, lanes_at(t, W)], out.at[b, m], zs.at[n, j], zr.at[n, j], (g, t)
        )

    def here(c):
        b = blocks_at(group(-c))
        return pltpu.make_async_copy(ebuf.at[b, :, lanes_at(m, W)], out.at[b, m], zl.at[ORDER.index(c)])

    def push(c):
        here(c).start()
        for j in (2, 1, 3):
            back(c, j).start()

    previous = None
    for c in ORDER:
        gr = group(-c)
        if c == 0:
            pltpu.make_async_copy(sbuf.at[g], tbuf.at[g], xl).wait()
            sources = [gr * BLK + (g + k) % BLK for k in range(1, BLK)]
        else:
            sources = [gr * BLK + k for k in range(BLK)]
        for s in sources:
            remote(sbuf.at[s], tbuf.at[s], xs.at[0], xr.at[s], (s, m)).wait_recv()

        def body(i, carry, gr=gr):
            blk = pl.ds(gr * BLK + 2 * i, 2)
            pair = (
                src[blk].reshape(128, D).astype(F32) * tbuf[blk].reshape(128, D).astype(F32)
            ).astype(BF)
            v = total[rows_at(gr * 4 + i, 128), :] + silu(dot(pair, edge_f[...]))
            ebuf[blk] = v.astype(BF).reshape(2, Q, D)
            return carry

        lax.fori_loop(0, BLK // 2, body, 0)
        push(c)
    for c in ORDER:
        here(c).wait()
        for j in (2, 1, 3):
            back(c, j).wait()
        for n, d in others(c):
            block_copy(n, d).wait_send()


def vmem(shape, dtype):
    return pltpu.VMEM(shape, dtype)


def run(kernel, outs, scratch, cid, name, args):
    spec = pl.BlockSpec(memory_space=pltpu.VMEM)
    return pl.pallas_call(
        kernel,
        out_shape=tuple(jax.ShapeDtypeStruct(s, d) for s, d in outs),
        in_specs=[spec] * len(args),
        out_specs=tuple([spec] * len(outs)),
        scratch_shapes=scratch,
        compiler_params=pltpu.CompilerParams(
            collective_id=cid, has_side_effects=True, vmem_limit_bytes=56 << 20
        ),
        name=name,
    )(*args)


def local(
    edge_feats,
    edge_source,
    edge_target,
    edge_live,
    trip_partner,
    trip_mask,
    trip_basis,
    atom_feats,
    w_msg,
    w_down,
    w_bil,
    w_up,
    w_atom,
    w_edge,
):
    n_edges = edge_feats.shape[0]
    n_atoms = atom_feats.shape[0]
    rows = n_edges // MP
    quarter = n_atoms // MP
    dma = pltpu.SemaphoreType.DMA
    l_mat = jnp.transpose(jnp.concatenate([w_bil[: 8 * DT], w_bil[8 * DT :]], axis=1))
    total, incoming, in_ids, atom_f, edge_f, arow = run(
        message_kernel,
        [
            ((rows, D), F32),
            ((NG, Q, D), BF),
            ((NG, 1, 128), jnp.int32),
            ((D, D), BF),
            ((D, D), BF),
            ((quarter, D), BF),
        ],
        [
            vmem((NG, Q, D), BF),
            vmem((NG // 2, CAP, 128), BF),
            vmem((NG, CAP, NB * Q), BF),
            vmem((64, 16, 128), BF),
            vmem((NG, Q, D), BF),
            vmem((NG, 1, 128), jnp.int32),
            vmem((D, D), BF),
            vmem((DT, D), BF),
            dma((13, 4)),
            dma((13, 4)),
            dma((13,)),
            dma((2, NG)),
            dma((2, NG)),
            dma((2,)),
        ],
        0,
        "messages",
        (
            edge_feats.reshape(NG, MP, Q, W),
            edge_target.reshape(2 * NG, 128),
            edge_live.reshape(2 * NG, 128),
            trip_partner,
            trip_mask,
            trip_basis.reshape(NG, MP, Q, 128),
            w_msg,
            w_down,
            l_mat,
            w_up,
            w_atom,
            w_edge,
            atom_feats.reshape(MP, quarter, W),
        ),
    )
    afull, aout = run(
        atom_kernel,
        [((n_atoms, D), BF), ((n_atoms, W), BF)],
        [
            vmem((NG // 2, 128), jnp.int32),
            vmem((MP, quarter, D), BF),
            vmem((MP, quarter, D), BF),
            vmem((quarter, D), F32),
            vmem((quarter // 2, rows), BF),
            dma((4, 2)),
            dma((4, 2)),
            dma((3, 2)),
            dma((3, 2)),
        ],
        1,
        "atoms",
        (incoming.reshape(rows, D), in_ids, arow, atom_f),
    )
    (edge_out,) = run(
        edge_kernel,
        [((NG, MP, Q, W), BF)],
        [
            vmem((BLK * Q, n_atoms), BF),
            vmem((NG, Q, D), BF),
            vmem((NG, Q, D), BF),
            vmem((NG, Q, D), BF),
            vmem((NG, Q, D), BF),
            dma((NG,)),
            dma((NG,)),
            dma,
            dma((4, 4)),
            dma((4, 4)),
            dma((4,)),
        ],
        2,
        "edges",
        (afull, in_ids, edge_source.reshape(2 * NG, 128), total, edge_f),
    )
    return (edge_out.reshape(n_edges, W), aout)


def solution(mesh):
    return jax.shard_map(
        local,
        mesh=mesh,
        in_specs=(
            P("graph", "mp"),
            P("graph"),
            P("graph"),
            P("graph"),
            P(None, "graph"),
            P(None, "graph"),
            P("graph", None),
            P("graph", "mp"),
            P(None, "mp"),
            P(),
            P(),
            P(None, "mp"),
            P(None, "mp"),
            P(None, "mp"),
        ),
        out_specs=(P("graph", "mp"), P("graph", "mp")),
        check_vma=False,
    )
```

```python
import jax
import jax.numpy as jnp
from jax import lax
from jax.experimental import pallas as pl
from jax.experimental.pallas import tpu as pltpu
from jax.sharding import PartitionSpec as P

DT = 64
NB = 16
SLOTS = 8
CAP = 256
MP = 4
Q = CAP // MP
NG = 32
BLK = 8
D = 512
W = D // MP
ORDER = (1, 3, 0, 2)
NEAR = (2, 1, 3, 0)
BF = jnp.bfloat16
F32 = jnp.float32
MESH = pl.DeviceIdType.MESH


def silu(v):
    h = 0.5 * v
    return h + h * jnp.tanh(h)


def dot(a, b):
    return jnp.dot(a, b, preferred_element_type=F32)


def lanes_at(k, n):
    return pl.ds(pl.multiple_of(k * n, n), n)


def rows_at(k, n):
    return pl.ds(pl.multiple_of(k * n, n), n)


def enter(g, m, over_graph):
    sem = pltpu.get_barrier_semaphore()
    peers = [(g, (m + k) % MP) for k in range(1, MP)]
    if over_graph:
        peers += [((g + k) % NG, m) for k in range(1, NG)]
    for peer in peers:
        pl.semaphore_signal(sem, inc=1, device_id=peer, device_id_type=MESH)
    pl.semaphore_wait(sem, len(peers))


def remote(src, dst, send, recv, peer):
    return pltpu.make_async_remote_copy(
        src_ref=src, dst_ref=dst, send_sem=send, recv_sem=recv, device_id=peer, device_id_type=MESH
    )


def low_lanes(shape):
    return lax.broadcasted_iota(jnp.int32, shape, len(shape) - 1) < Q


def pair_row(ref, blk, m):
    half = m // 2
    a = ref[pl.ds(2 * blk + half, 1), :]
    b = ref[pl.ds(2 * blk + 2 + half, 1), :]
    odd = m % 2 == 1
    ra, rb = pltpu.roll(a, Q, 1), pltpu.roll(b, Q, 1)
    return jnp.where(low_lanes(a.shape), jnp.where(odd, ra, a), jnp.where(odd, b, rb))


def column(row):
    return jnp.transpose(jnp.broadcast_to(row.astype(F32), (128, 128)))


def block_kernel(
    ef,
    target,
    live,
    source,
    partner,
    mask,
    basis,
    w_msg,
    w_down_t,
    w_bil_t,
    w_up,
    w_atom,
    w_edge,
    af,
    out,
    aout,
    x,
    dall,
    at,
    wrow,
    mix,
    l_mat,
    total,
    outg,
    incoming,
    tbuf,
    idq,
    in_ids,
    idr,
    wf,
    up_f,
    hot,
    tmp,
    part_f,
    own,
    pbuf,
    rbuf,
    afull,
    srcb,
    es,
    er,
    el,
    ds,
    dr,
    ws,
    wr,
    wl,
    vs,
    vr,
    xs,
    xr,
    xl,
    ps,
    pr,
    us,
    ur,
    zs,
    zr,
    zl,
):
    g = lax.axis_index("graph")
    m = lax.axis_index("mp")
    cx, cy, core = g // 8, (g // 2) % 4, g % 2
    quarter = own.shape[0]
    h2 = quarter // 2
    n_atoms = afull.shape[0]
    up, dn, op = (m + 1) % MP, (m + 3) % MP, (m + 2) % MP

    def to_pair(k, i):
        return ((cx + i) % 4) * 4 + (cy + k - i + 4) % 4

    def from_pair(k, i):
        return ((cx - i + 4) % 4) * 4 + (cy - k + i + 4) % 4

    def two(p):
        return pl.ds(2 * p, 2)

    enter(g, m, True)

    def ef_copy(k, i, j):
        p, n = to_pair(k, i), 4 * k + i
        t = (m + j) % MP
        return remote(ef.at[two(p), t], x.at[m, two(p)], es.at[n, j], er.at[n, j], (g, t))

    def ef_here(k, i):
        p = to_pair(k, i)
        return pltpu.make_async_copy(ef.at[two(p), m], x.at[m, two(p)], el.at[4 * k + i])

    def ef_start(k):
        for i in range(4):
            ef_here(k, i).start()
            for j in (2, 1, 3):
                ef_copy(k, i, j).start()

    def ef_wait(k):
        for i in range(4):
            ef_here(k, i).wait()
            for j in (2, 1, 3):
                ef_copy(k, i, j).wait_recv()

    def down_copy(k, i, j):
        p, n = to_pair(k, i), 4 * k + i
        d = dall.at[p, rows_at(m, Q), :]
        return remote(d, d, ds.at[n, j], dr.at[n, j], (g, (m + j) % MP))

    def down_start(k):
        for i in range(4):
            for j in (2, 1, 3):
                down_copy(k, i, j).start()

    def down_wait(k):
        for i in range(4):
            for j in (2, 1, 3):
                down_copy(k, i, j).wait_recv()

    weights = (w_msg, w_atom, w_edge)
    piece = pl.ds(pl.multiple_of(16 * g, 16), 16)

    def w_copy(n, j):
        peer = (g, (m + j) % MP)
        if n == 3:
            return remote(w_up, up_f.at[m], ws.at[n, j], wr.at[n, j], peer)
        return remote(weights[n].at[piece], wf.at[n, m, piece], ws.at[n, j], wr.at[n, j], peer)

    def w_here(n):
        if n == 3:
            return pltpu.make_async_copy(w_up, up_f.at[m], wl.at[n])
        return pltpu.make_async_copy(weights[n].at[piece], wf.at[n, m, piece], wl.at[n])

    def w_spread(n, k):
        d = (g + k) % NG
        ref = wf.at[n, :, piece]
        return remote(ref, ref, vs.at[n, k], vr.at[n, g], (d, m))

    def w_spread_wait(n):
        for k in range(1, NG):
            s = (g + k) % NG
            ref = wf.at[n, :, pl.ds(pl.multiple_of(16 * s, 16), 16)]
            remote(ref, ref, vs.at[n, k], vr.at[n, s], (s, m)).wait_recv()

    def w_full(n):
        return jnp.concatenate([wf[n, j] for j in range(MP)], axis=1)

    for n in range(4):
        w_here(n).start()
        for j in (2, 1, 3):
            w_copy(n, j).start()
    ef_start(ORDER[0])
    ef_start(ORDER[1])

    def write_ids(p, carry):
        row = pair_row(target, 2 * p, m) & 2047
        idq[2 * p] = row
        idq[2 * p + 1] = pltpu.roll(row, Q, 1)
        return carry

    lax.fori_loop(0, NG // 2, write_ids, 0)
    l_mat[:DT, :] = w_bil_t[:, : 8 * DT]
    l_mat[DT:, :] = w_bil_t[:, 8 * DT :]

    def weights_of(blk0):
        t = jnp.transpose(
            jnp.concatenate([basis[blk0, m], basis[blk0 + 1, m]], axis=0).astype(F32)
        ).reshape(SLOTS, 2, 8, 128)
        lo, hi = t[:, 0], t[:, 1]
        low = low_lanes((SLOTS, 8, 128))
        return (
            jnp.where(low, lo, pltpu.roll(hi.reshape(64, 128), Q, 1).reshape(SLOTS, 8, 128)),
            jnp.where(low, pltpu.roll(lo.reshape(64, 128), Q, 1).reshape(SLOTS, 8, 128), hi),
        )

    def ids_of(blk):
        cols = lanes_at(2 * blk + m // 2, 128)
        v = jnp.where(mask[:, cols] != 0, partner[:, cols] & 255, -1)
        r = pltpu.roll(v, Q, 1)
        odd = m % 2 == 1
        low = low_lanes(v.shape)
        return jnp.where(low, jnp.where(odd, r, v), jnp.where(odd, v, r))

    def spread(k):
        def body(i, carry):
            blk0 = 2 * to_pair(k, i)
            both = weights_of(blk0)
            for half in range(2):
                blk = blk0 + half
                w = both[half]
                for s in range(SLOTS):
                    for j in range(8):
                        wrow[s * 8 + j] = jnp.broadcast_to(w[s, j : j + 1, :], (16, 128)).astype(BF)
                ids = ids_of(blk)

                def part(pt, carry):
                    p_ids = lax.broadcasted_iota(jnp.int32, (32, 128), 0) + 32 * pt
                    acc = [jnp.zeros((2, 16, 128), BF) for _ in range(8)]
                    for s in range(SLOTS):
                        same = (
                            jnp.where(ids[s : s + 1, :] == p_ids, 1.0, 0.0)
                            .astype(BF)
                            .reshape(2, 16, 128)
                        )
                        for j in range(8):
                            acc[j] = acc[j] + same * wrow[s * 8 + j][None]
                    for j in range(8):
                        at[blk, rows_at(pt, 32), 128 * j : 128 * (j + 1)] = acc[j].reshape(32, 128)
                    return carry

                lax.fori_loop(0, 8, part, 0)
            return carry

        lax.fori_loop(0, 4, body, 0)

    def rows_of_x(p):
        return jnp.concatenate([x[j, two(p)].reshape(128, W) for j in range(MP)], axis=1)

    def down(k):
        def body(i, carry):
            p = to_pair(k, i)
            d = lax.dot_general(
                rows_of_x(p), w_down_t[...], (((1,), (1,)), ((), ())), preferred_element_type=F32
            )
            dall[p, rows_at(m, Q), :] = jnp.concatenate([d[:Q], d[Q:]], axis=1).astype(BF)
            return carry

        lax.fori_loop(0, 4, body, 0)

    def hidden(k):
        def body(i, carry):
            p = to_pair(k, i)
            rows = rows_of_x(p)
            total[rows_at(p, 128), :] = rows.astype(F32) + silu(dot(rows, w_full(0)))
            return carry

        lax.fori_loop(0, 4, body, 0)

    def finish(k):
        for i in range(4):
            p = to_pair(k, i)
            dt = jnp.transpose(dall[p].astype(F32)).astype(BF)
            for half in range(2):
                mixed = dot(dt[half * DT : (half + 1) * DT], at[2 * p + half]).astype(BF)
                mix[:, 256 * i + 128 * half : 256 * i + 128 * (half + 1)] = jnp.concatenate(
                    [mixed[:, 128 * j : 128 * (j + 1)] for j in range(8)], axis=0
                )
        o = dot(l_mat[...], mix[...])
        low = low_lanes((DT, 128))
        parts = []
        for i in range(4):
            a, b = o[:, 256 * i : 256 * i + 128], o[:, 256 * i + 128 : 256 * (i + 1)]
            parts.append(
                jnp.where(low, a[:DT] + pltpu.roll(a[DT:], Q, 1), pltpu.roll(b[:DT], Q, 1) + b[DT:])
            )
        up_all = jnp.concatenate([up_f[j] for j in range(MP)], axis=1)
        bil = jnp.transpose(jnp.concatenate(parts, axis=1)).astype(BF)
        for i in range(4):
            p = to_pair(k, i)
            rows = rows_at(p, 128)
            tot = total[rows, :] + dot(bil[128 * i : 128 * (i + 1)], up_all)
            total[rows, :] = tot
            alive = column(pair_row(live, 2 * p, m))
            alive = jnp.concatenate([alive] * 4, axis=1)
            outg[two(p)] = (tot * alive).astype(BF).reshape(2, Q, D)

    def targets(k):
        found = []
        for i in NEAR:
            n = 2 * (4 * k + i)
            p = to_pair(k, i)
            if k == 0 and i == 0:
                found.append((n, 2 * p + 1 - core))
            else:
                found += [(n, 2 * p), (n + 1, 2 * p + 1)]
        return found

    def sources(k):
        found = []
        for i in NEAR:
            p = from_pair(k, i)
            if k == 0 and i == 0:
                found.append(2 * p + 1 - core)
            else:
                found += [2 * p, 2 * p + 1]
        return found

    def graph_copy(q, n, d):
        src, dst = ((outg, incoming), (outg, tbuf), (idq, in_ids))[q]
        return remote(src.at[d], dst.at[g], xs.at[q, n], xr.at[q, g], (d, m))

    def graph_here(q):
        src, dst = ((outg, incoming), (outg, tbuf), (idq, in_ids))[q]
        return pltpu.make_async_copy(src.at[g], dst.at[g], xl.at[q])

    def graph_send(q, k):
        if k == 0:
            graph_here(q).start()
        for n, d in targets(k):
            graph_copy(q, n, d).start()

    def graph_wait(q, k):
        src, dst = ((outg, incoming), (outg, tbuf), (idq, in_ids))[q]
        if k == 0:
            graph_here(q).wait()
        for s in sources(k):
            remote(src.at[s], dst.at[s], xs.at[q, 0], xr.at[q, s], (s, m)).wait_recv()

    def graph_sent(q):
        for k in range(4):
            for n, d in targets(k):
                graph_copy(q, n, d).wait_send()

    spread(ORDER[0])
    for n in range(4):
        w_here(n).wait()
        for j in (2, 1, 3):
            w_copy(n, j).wait_recv()
    for k in range(1, NG):
        w_spread(0, k).start()
    for k in ORDER:
        graph_send(2, k)
    spread(ORDER[1])
    ef_wait(ORDER[0])
    down(ORDER[0])
    down_start(ORDER[0])
    ef_start(ORDER[2])
    w_spread_wait(0)
    hidden(ORDER[0])
    spread(ORDER[2])
    ef_wait(ORDER[1])
    down(ORDER[1])
    down_start(ORDER[1])
    ef_start(ORDER[3])
    down_wait(ORDER[0])
    finish(ORDER[0])
    hidden(ORDER[1])
    graph_send(0, ORDER[0])
    spread(ORDER[3])
    ef_wait(ORDER[2])
    down(ORDER[2])
    down_start(ORDER[2])
    down_wait(ORDER[1])
    finish(ORDER[1])
    hidden(ORDER[2])
    graph_send(0, ORDER[1])
    ef_wait(ORDER[3])
    down(ORDER[3])
    down_start(ORDER[3])
    down_wait(ORDER[2])
    finish(ORDER[2])
    hidden(ORDER[3])
    graph_send(0, ORDER[2])
    down_wait(ORDER[3])
    finish(ORDER[3])
    for k in ORDER:
        graph_wait(2, k)

    def pairs(i, carry):
        a, b = in_ids[2 * i], in_ids[2 * i + 1]
        idr[pl.ds(i, 1), :] = jnp.where(low_lanes(a.shape), a, pltpu.roll(b, Q, 1))
        return carry

    lax.fori_loop(0, NG // 2, pairs, 0)
    graph_send(0, ORDER[3])
    for n in (1, 2):
        for k in range(1, NG):
            w_spread(n, k).start()

    def hot_rows(slot, p, row):
        col = column(row)
        for k in range(n_atoms // 128):
            lane = lax.broadcasted_iota(jnp.int32, (128, 128), 1).astype(F32) + 128.0 * k
            at[slot, 128 * (k // 8) : 128 * (k // 8) + 128, 128 * (k % 8) : 128 * (k % 8) + 128] = (
                jnp.where(col == lane, 1.0, 0.0).astype(BF)
            )

    def hot_targets(k):
        def body(i, carry):
            p = to_pair(k, i)
            hot_rows(4 * k + i, p, idr[pl.ds(p, 1), :])
            return carry

        lax.fori_loop(0, 4, body, 0)

    def hot_sources(k):
        def body(i, carry):
            p = from_pair(k, i)
            hot_rows(16 + 4 * k + i, p, pair_row(source, 2 * p, m) & 2047)
            return carry

        lax.fori_loop(0, 4, body, 0)

    for k in ORDER:
        graph_wait(0, k)

    def part(t, h):
        base = t * quarter + h * h2

        def build(i, carry):
            ids = lax.broadcasted_iota(jnp.int32, (h2, 128), 0) + base
            hot[:, lanes_at(i, 128)] = jnp.where(idr[pl.ds(i, 1), :] == ids, 1.0, 0.0).astype(BF)
            return carry

        lax.fori_loop(0, NG // 2, build, 0)
        tmp[...] = dot(hot[...], incoming[...].reshape(NG * Q, D))
        own_lanes = lanes_at(m, W)
        tmp[:, own_lanes] = tmp[:, own_lanes] + af[
            pl.ds(pl.multiple_of(base, h2), h2), :
        ].astype(F32)
        return tmp[...]

    def p_copy(n):
        t = (up, dn, up, dn, up, dn)[n]
        return remote(pbuf.at[n], rbuf.at[n], ps.at[n], pr.at[n], (g, t))

    pbuf[0] = part(op, 0).astype(BF)
    pbuf[1] = part(op, 1).astype(BF)
    p_copy(0).start()
    part_f[0] = part(up, 0)
    p_copy(1).start()
    part_f[1] = part(dn, 1)
    pbuf[2] = part(up, 1).astype(BF)
    pbuf[3] = part(dn, 0).astype(BF)
    p_copy(2).start()
    p_copy(0).wait_recv()
    pbuf[4] = (part_f[0] + rbuf[0].astype(F32)).astype(BF)
    p_copy(3).start()
    p_copy(1).wait_recv()
    pbuf[5] = (part_f[1] + rbuf[1].astype(F32)).astype(BF)
    p_copy(4).start()
    own[:h2, :] = part(m, 0)
    p_copy(5).start()
    own[h2:, :] = part(m, 1)
    for k in ORDER:
        hot_targets(k)
    w_spread_wait(1)
    graph_sent(0)

    def rows_of(src, h):
        return afull.at[pl.ds(pl.multiple_of(src * quarter + h * h2, h2), h2)]

    def own_copy(h, to):
        t = up if to == 0 else dn
        return remote(rows_of(m, h), rows_of(m, h), us.at[to, h], ur.at[to, h], (g, t))

    def relay(to):
        src, t = (dn, up) if to == 0 else (up, dn)
        return remote(rows_of(src, to), rows_of(src, to), us.at[2, to], ur.at[2, to], (g, t))

    for h in range(2):
        rows = slice(h * h2, (h + 1) * h2)
        a, b = ((3, 4), (2, 5))[h]
        p_copy(a).wait_recv()
        p_copy(b).wait_recv()
        mid = (own[rows, :] + rbuf[a].astype(F32) + rbuf[b].astype(F32)).astype(BF)
        new = (mid.astype(F32) + silu(dot(mid, w_full(1)))).astype(BF)
        afull[pl.ds(pl.multiple_of(m * quarter + h * h2, h2), h2), :] = new
        for to in (h, 1 - h):
            own_copy(h, to).start()
    hot_sources(ORDER[0])
    own_copy(0, 0).wait_recv()
    relay(0).start()
    own_copy(1, 1).wait_recv()
    relay(1).start()
    for k in ORDER[1:]:
        hot_sources(k)
    w_spread_wait(2)
    own_copy(0, 1).wait_recv()
    own_copy(1, 0).wait_recv()
    relay(0).wait_recv()
    relay(1).wait_recv()

    def pick(slot):
        n2 = n_atoms // 2
        hots = at[slot : slot + 4]
        return (
            dot(hots[:, :128].reshape(512, n2), afull[:n2, :])
            + dot(hots[:, 128:].reshape(512, n2), afull[n2:, :])
        ).astype(BF)

    previous = None
    for k in ORDER:
        v = pick(4 * k).reshape(4, 2, Q, D)
        for i in range(4):
            outg[two(to_pair(k, i))] = v[i]
        if previous is not None:
            graph_send(1, previous)
        previous = k
    srcb[...] = pick(16 + 4 * ORDER[0]).reshape(4, 128, D)
    graph_send(1, previous)

    def back(k, i, j):
        p, n = from_pair(k, i), 4 * k + i
        t = (m + j) % MP
        return remote(x.at[t, two(p)], out.at[two(p), m], zs.at[n, j], zr.at[n, j], (g, t))

    def here(k, i):
        p = from_pair(k, i)
        return pltpu.make_async_copy(x.at[m, two(p)], out.at[two(p), m], zl.at[4 * k + i])

    for n, k in enumerate(ORDER):
        if n > 0:
            srcb[...] = pick(16 + 4 * k).reshape(4, 128, D)
        if n == 1:
            aout[...] = afull[:, lanes_at(m, W)]
        graph_wait(1, k)

        def body(i, carry, k=k):
            p = from_pair(k, i)
            pair = (srcb[i].astype(F32) * tbuf[two(p)].reshape(128, D).astype(F32)).astype(BF)
            v = (total[rows_at(p, 128), :] + silu(dot(pair, w_full(2)))).astype(BF)
            for j in range(MP):
                x[j, two(p)] = v[:, W * j : W * (j + 1)].reshape(2, Q, W)
            return carry

        lax.fori_loop(0, 4, body, 0)
        for i in range(4):
            here(k, i).start()
            for j in (2, 1, 3):
                back(k, i, j).start()
    for k in ORDER:
        for i in range(4):
            here(k, i).wait()
            for j in (2, 1, 3):
                back(k, i, j).wait()
                ef_copy(k, i, j).wait_send()
                down_copy(k, i, j).wait_send()
    for n in range(4):
        for j in (2, 1, 3):
            w_copy(n, j).wait_send()
    for n in range(3):
        for k in range(1, NG):
            w_spread(n, k).wait_send()
    graph_sent(1)
    graph_sent(2)
    for n in range(6):
        p_copy(n).wait_send()
    for h in range(2):
        for to in range(2):
            own_copy(h, to).wait_send()
        relay(h).wait_send()


def vmem(shape, dtype):
    return pltpu.VMEM(shape, dtype)


def local(
    edge_feats,
    edge_source,
    edge_target,
    edge_live,
    trip_partner,
    trip_mask,
    trip_basis,
    atom_feats,
    w_msg,
    w_down,
    w_bil,
    w_up,
    w_atom,
    w_edge,
):
    n_edges = edge_feats.shape[0]
    n_atoms = atom_feats.shape[0]
    rows = n_edges // MP
    quarter = n_atoms // MP
    half = quarter // 2
    dma = pltpu.SemaphoreType.DMA
    args = (
        edge_feats.reshape(NG, MP, Q, W),
        edge_target.reshape(2 * NG, 128),
        edge_live.reshape(2 * NG, 128),
        edge_source.reshape(2 * NG, 128),
        trip_partner,
        trip_mask,
        trip_basis.reshape(NG, MP, Q, 128),
        w_msg,
        jnp.transpose(w_down),
        jnp.transpose(w_bil),
        w_up,
        w_atom,
        w_edge,
        atom_feats,
    )
    spec = pl.BlockSpec(memory_space=pltpu.VMEM)
    edge_out, aout = pl.pallas_call(
        block_kernel,
        out_shape=(
            jax.ShapeDtypeStruct((NG, MP, Q, W), BF),
            jax.ShapeDtypeStruct((n_atoms, W), BF),
        ),
        in_specs=[spec] * len(args),
        out_specs=(spec, spec),
        scratch_shapes=[
            vmem((MP, NG, Q, W), BF),
            vmem((NG // 2, CAP, 128), BF),
            vmem((NG, CAP, NB * Q), BF),
            vmem((64, 16, 128), BF),
            vmem((8 * DT, 1024), BF),
            vmem((128, 8 * DT), BF),
            vmem((rows, D), F32),
            vmem((NG, Q, D), BF),
            vmem((NG, Q, D), BF),
            vmem((NG, Q, D), BF),
            vmem((NG, 1, 128), jnp.int32),
            vmem((NG, 1, 128), jnp.int32),
            vmem((NG // 2, 128), jnp.int32),
            vmem((3, MP, D, W), BF),
            vmem((MP, DT, W), BF),
            vmem((half, rows), BF),
            vmem((half, D), F32),
            vmem((2, half, D), F32),
            vmem((quarter, D), F32),
            vmem((6, half, D), BF),
            vmem((6, half, D), BF),
            vmem((n_atoms, D), BF),
            vmem((4, 128, D), BF),
            dma((16, 4)),
            dma((16, 4)),
            dma((16,)),
            dma((16, 4)),
            dma((16, 4)),
            dma((4, 4)),
            dma((4, 4)),
            dma((4,)),
            dma((3, NG)),
            dma((3, NG)),
            dma((3, NG)),
            dma((3, NG)),
            dma((3,)),
            dma((6,)),
            dma((6,)),
            dma((3, 2)),
            dma((3, 2)),
            dma((16, 4)),
            dma((16, 4)),
            dma((16,)),
        ],
        compiler_params=pltpu.CompilerParams(
            collective_id=0, has_side_effects=True, vmem_limit_bytes=62 << 20
        ),
        name="block",
    )(*args)
    return (edge_out.reshape(n_edges, W), aout)


def solution(mesh):
    return jax.shard_map(
        local,
        mesh=mesh,
        in_specs=(
            P("graph", "mp"),
            P("graph"),
            P("graph"),
            P("graph"),
            P(None, "graph"),
            P(None, "graph"),
            P("graph", None),
            P("graph", "mp"),
            P(None, "mp"),
            P(),
            P(),
            P(None, "mp"),
            P(None, "mp"),
            P(None, "mp"),
        ),
        out_specs=(P("graph", "mp"), P("graph", "mp")),
        check_vma=False,
    )
```

```python
import jax
import jax.numpy as jnp
from jax import lax
from jax.experimental import pallas as pl
from jax.experimental.pallas import tpu as pltpu
from jax.sharding import PartitionSpec as P

DT = 64
NB = 16
SLOTS = 8
CAP = 256
MP = 4
Q = CAP // MP
NG = 32
BLK = 8
D = 512
W = D // MP
ORDER = (1, 3, 0, 2)
NEAR = (2, 1, 3, 0)
BF = jnp.bfloat16
F32 = jnp.float32
MESH = pl.DeviceIdType.MESH


def silu(v):
    h = 0.5 * v
    return h + h * jnp.tanh(h)


def dot(a, b):
    return jnp.dot(a, b, preferred_element_type=F32)


def lanes_at(k, n):
    return pl.ds(pl.multiple_of(k * n, n), n)


def rows_at(k, n):
    return pl.ds(pl.multiple_of(k * n, n), n)


def enter(g, m, over_graph):
    sem = pltpu.get_barrier_semaphore()
    peers = [(g, (m + k) % MP) for k in range(1, MP)]
    if over_graph:
        peers += [((g + k) % NG, m) for k in range(1, NG)]
    for peer in peers:
        pl.semaphore_signal(sem, inc=1, device_id=peer, device_id_type=MESH)
    pl.semaphore_wait(sem, len(peers))


def remote(src, dst, send, recv, peer):
    return pltpu.make_async_remote_copy(
        src_ref=src, dst_ref=dst, send_sem=send, recv_sem=recv, device_id=peer, device_id_type=MESH
    )


def low_lanes(shape):
    return lax.broadcasted_iota(jnp.int32, shape, len(shape) - 1) < Q


def pair_row(ref, blk, m):
    half = m // 2
    a = ref[pl.ds(2 * blk + half, 1), :]
    b = ref[pl.ds(2 * blk + 2 + half, 1), :]
    odd = m % 2 == 1
    ra, rb = pltpu.roll(a, Q, 1), pltpu.roll(b, Q, 1)
    return jnp.where(low_lanes(a.shape), jnp.where(odd, ra, a), jnp.where(odd, b, rb))


def column(row):
    return jnp.transpose(jnp.broadcast_to(row.astype(F32), (128, 128)))


def block_kernel(
    ef,
    target,
    live,
    source,
    partner,
    mask,
    basis,
    w_msg,
    w_down_t,
    w_bil_t,
    w_up,
    w_atom,
    w_edge,
    af,
    out,
    aout,
    x,
    dall,
    at,
    wrow,
    irow,
    mix,
    l_mat,
    total,
    outg,
    incoming,
    tbuf,
    idq,
    in_ids,
    idr,
    wf,
    up_f,
    hot,
    pacc,
    part_f,
    own,
    pbuf,
    rbuf,
    afull,
    srcb,
    basis_v,
    partner_v,
    mask_v,
    af_v,
    il,
    es,
    er,
    el,
    ds,
    dr,
    ws,
    wr,
    wl,
    vs,
    vr,
    xs,
    xr,
    xl,
    ps,
    pr,
    us,
    ur,
    zs,
    zr,
    zl,
):
    g = lax.axis_index("graph")
    m = lax.axis_index("mp")
    cx, cy, core = g // 8, (g // 2) % 4, g % 2
    quarter = own.shape[0]
    h2 = quarter // 2
    n_atoms = afull.shape[0]
    up, dn, op = (m + 1) % MP, (m + 3) % MP, (m + 2) % MP

    def to_pair(k, i):
        return ((cx + i) % 4) * 4 + (cy + k - i + 4) % 4

    def from_pair(k, i):
        return ((cx - i + 4) % 4) * 4 + (cy - k + i + 4) % 4

    def two(p):
        return pl.ds(2 * p, 2)

    loads = (
        (basis.at[:, m], basis_v),
        (partner, partner_v),
        (mask, mask_v),
        (af, af_v),
    )

    def load(n):
        return pltpu.make_async_copy(loads[n][0], loads[n][1], il.at[n])

    for n in range(4):
        load(n).start()
    enter(g, m, True)

    def ef_copy(k, i, j):
        p, n = to_pair(k, i), 4 * k + i
        t = (m + j) % MP
        return remote(ef.at[two(p), t], x.at[m, two(p)], es.at[n, j], er.at[n, j], (g, t))

    def ef_here(k, i):
        p = to_pair(k, i)
        return pltpu.make_async_copy(ef.at[two(p), m], x.at[m, two(p)], el.at[4 * k + i])

    def ef_start(k):
        for i in range(4):
            ef_here(k, i).start()
            for j in (2, 1, 3):
                ef_copy(k, i, j).start()

    def ef_wait(k):
        for i in range(4):
            ef_here(k, i).wait()
            for j in (2, 1, 3):
                ef_copy(k, i, j).wait_recv()

    def down_copy(k, i, j):
        p, n = to_pair(k, i), 4 * k + i
        d = dall.at[p, rows_at(m, Q), :]
        return remote(d, d, ds.at[n, j], dr.at[n, j], (g, (m + j) % MP))

    def down_start(k):
        for i in range(4):
            for j in (2, 1, 3):
                down_copy(k, i, j).start()

    def down_wait(k):
        for i in range(4):
            for j in (2, 1, 3):
                down_copy(k, i, j).wait_recv()

    weights = (w_msg, w_atom, w_edge)
    piece = pl.ds(pl.multiple_of(16 * g, 16), 16)

    def w_copy(n, j):
        peer = (g, (m + j) % MP)
        if n == 3:
            return remote(w_up, up_f.at[m], ws.at[n, j], wr.at[n, j], peer)
        return remote(weights[n].at[piece], wf.at[n, m, piece], ws.at[n, j], wr.at[n, j], peer)

    def w_here(n):
        if n == 3:
            return pltpu.make_async_copy(w_up, up_f.at[m], wl.at[n])
        return pltpu.make_async_copy(weights[n].at[piece], wf.at[n, m, piece], wl.at[n])

    def w_spread(n, k):
        d = (g + k) % NG
        ref = wf.at[n, :, piece]
        return remote(ref, ref, vs.at[n, k], vr.at[n, g], (d, m))

    def w_spread_wait(n):
        for k in range(1, NG):
            s = (g + k) % NG
            ref = wf.at[n, :, pl.ds(pl.multiple_of(16 * s, 16), 16)]
            remote(ref, ref, vs.at[n, k], vr.at[n, s], (s, m)).wait_recv()

    def w_full(n):
        return jnp.concatenate([wf[n, j] for j in range(MP)], axis=1)

    for n in range(4):
        w_here(n).start()
        for j in (2, 1, 3):
            w_copy(n, j).start()
    ef_start(ORDER[0])
    ef_start(ORDER[1])

    def write_ids(p, carry):
        row = pair_row(target, 2 * p, m) & 2047
        idq[2 * p] = row
        idq[2 * p + 1] = pltpu.roll(row, Q, 1)
        return carry

    lax.fori_loop(0, NG // 2, write_ids, 0)
    l_mat[:DT, :] = w_bil_t[:, : 8 * DT]
    l_mat[DT:, :] = w_bil_t[:, 8 * DT :]

    def weights_of(blk0):
        t = jnp.transpose(
            basis_v[pl.ds(blk0, 2)].reshape(128, 128).astype(F32)
        ).reshape(SLOTS, 2, 8, 128)
        lo, hi = t[:, 0], t[:, 1]
        low = low_lanes((SLOTS, 8, 128))
        return (
            jnp.where(low, lo, pltpu.roll(hi.reshape(64, 128), Q, 1).reshape(SLOTS, 8, 128)),
            jnp.where(low, pltpu.roll(lo.reshape(64, 128), Q, 1).reshape(SLOTS, 8, 128), hi),
        )

    def ids_of(blk):
        cols = lanes_at(2 * blk + m // 2, 128)
        v = jnp.where(mask_v[:, cols] != 0, partner_v[:, cols] & 255, -1)
        r = pltpu.roll(v, Q, 1)
        odd = m % 2 == 1
        low = low_lanes(v.shape)
        return jnp.where(low, jnp.where(odd, r, v), jnp.where(odd, v, r))

    def spread(k):
        one, zero = jnp.ones((2, 16, 128), BF), jnp.zeros((2, 16, 128), BF)

        def body(i, carry):
            blk0 = 2 * to_pair(k, i)
            both = weights_of(blk0)
            for half in range(2):
                blk = blk0 + half
                w = both[half]
                for s in range(SLOTS):
                    for j in range(8):
                        wrow[s * 8 + j] = jnp.broadcast_to(w[s, j : j + 1, :], (16, 128)).astype(BF)
                ids = ids_of(blk).astype(F32)
                for s in range(SLOTS):
                    irow[s] = jnp.broadcast_to(ids[s : s + 1, :], (16, 128)).astype(BF)

                def part(pt, carry):
                    p_ids = (
                        (lax.broadcasted_iota(jnp.int32, (32, 128), 0) + 32 * pt)
                        .astype(F32)
                        .astype(BF)
                        .reshape(2, 16, 128)
                    )
                    acc = [None] * 8
                    for s in range(SLOTS):
                        same = jnp.where(irow[s][None] == p_ids, one, zero)
                        for j in range(8):
                            term = same * wrow[s * 8 + j][None]
                            acc[j] = term if s == 0 else acc[j] + term
                    for j in range(8):
                        at[blk, rows_at(pt, 32), 128 * j : 128 * (j + 1)] = acc[j].reshape(32, 128)
                    return carry

                lax.fori_loop(0, 8, part, 0)
            return carry

        lax.fori_loop(0, 4, body, 0)

    def rows_of_x(p):
        return jnp.concatenate([x[j, two(p)].reshape(128, W) for j in range(MP)], axis=1)

    def down(k):
        def body(i, carry):
            p = to_pair(k, i)
            d = lax.dot_general(
                rows_of_x(p), w_down_t[...], (((1,), (1,)), ((), ())), preferred_element_type=F32
            )
            dall[p, rows_at(m, Q), :] = jnp.concatenate([d[:Q], d[Q:]], axis=1).astype(BF)
            return carry

        lax.fori_loop(0, 4, body, 0)

    def hidden(k):
        def body(i, carry):
            p = to_pair(k, i)
            rows = rows_of_x(p)
            total[rows_at(p, 128), :] = rows.astype(F32) + silu(dot(rows, w_full(0)))
            return carry

        lax.fori_loop(0, 4, body, 0)

    def finish(k):
        for i in range(4):
            p = to_pair(k, i)
            dt = jnp.transpose(dall[p].astype(F32)).astype(BF)
            for half in range(2):
                mixed = dot(dt[half * DT : (half + 1) * DT], at[2 * p + half]).astype(BF)
                mix[:, 256 * i + 128 * half : 256 * i + 128 * (half + 1)] = jnp.concatenate(
                    [mixed[:, 128 * j : 128 * (j + 1)] for j in range(8)], axis=0
                )
        o = dot(l_mat[...], mix[...])
        low = low_lanes((DT, 128))
        parts = []
        for i in range(4):
            a, b = o[:, 256 * i : 256 * i + 128], o[:, 256 * i + 128 : 256 * (i + 1)]
            parts.append(
                jnp.where(low, a[:DT] + pltpu.roll(a[DT:], Q, 1), pltpu.roll(b[:DT], Q, 1) + b[DT:])
            )
        up_all = jnp.concatenate([up_f[j] for j in range(MP)], axis=1)
        bil = jnp.transpose(jnp.concatenate(parts, axis=1)).astype(BF)
        for i in range(4):
            p = to_pair(k, i)
            rows = rows_at(p, 128)
            tot = total[rows, :] + dot(bil[128 * i : 128 * (i + 1)], up_all)
            total[rows, :] = tot
            alive = column(pair_row(live, 2 * p, m))
            alive = jnp.concatenate([alive] * 4, axis=1)
            outg[two(p)] = (tot * alive).astype(BF).reshape(2, Q, D)

    def targets(k):
        found = []
        for i in NEAR:
            n = 2 * (4 * k + i)
            p = to_pair(k, i)
            if k == 0 and i == 0:
                found.append((n, 2 * p + 1 - core))
            else:
                found += [(n, 2 * p), (n + 1, 2 * p + 1)]
        return found

    def sources(k):
        found = []
        for i in NEAR:
            p = from_pair(k, i)
            if k == 0 and i == 0:
                found.append(2 * p + 1 - core)
            else:
                found += [2 * p, 2 * p + 1]
        return found

    def graph_copy(q, n, d):
        src, dst = ((outg, incoming), (outg, tbuf), (idq, in_ids))[q]
        return remote(src.at[d], dst.at[g], xs.at[q, n], xr.at[q, g], (d, m))

    def graph_here(q):
        src, dst = ((outg, incoming), (outg, tbuf), (idq, in_ids))[q]
        return pltpu.make_async_copy(src.at[g], dst.at[g], xl.at[q])

    def graph_send(q, k):
        if k == 0:
            graph_here(q).start()
        for n, d in targets(k):
            graph_copy(q, n, d).start()

    def graph_wait(q, k):
        src, dst = ((outg, incoming), (outg, tbuf), (idq, in_ids))[q]
        if k == 0:
            graph_here(q).wait()
        for s in sources(k):
            remote(src.at[s], dst.at[s], xs.at[q, 0], xr.at[q, s], (s, m)).wait_recv()

    def graph_sent(q, k):
        for n, d in targets(k):
            graph_copy(q, n, d).wait_send()

    for n in range(3):
        load(n).wait()
    spread(ORDER[0])
    for n in range(4):
        w_here(n).wait()
        for j in (2, 1, 3):
            w_copy(n, j).wait_recv()
    for k in range(1, NG):
        w_spread(0, k).start()
    for k in ORDER:
        graph_send(2, k)
    ef_wait(ORDER[0])
    down(ORDER[0])
    down_start(ORDER[0])
    ef_start(ORDER[2])
    spread(ORDER[1])
    w_spread_wait(0)
    hidden(ORDER[0])
    ef_wait(ORDER[1])
    down(ORDER[1])
    down_start(ORDER[1])
    ef_start(ORDER[3])
    down_wait(ORDER[0])
    finish(ORDER[0])
    hidden(ORDER[1])
    graph_send(0, ORDER[0])
    spread(ORDER[2])
    ef_wait(ORDER[2])
    down(ORDER[2])
    down_start(ORDER[2])
    down_wait(ORDER[1])
    finish(ORDER[1])
    hidden(ORDER[2])
    graph_send(0, ORDER[1])
    spread(ORDER[3])
    ef_wait(ORDER[3])
    down(ORDER[3])
    down_start(ORDER[3])
    for k in ORDER:
        graph_wait(2, k)
    down_wait(ORDER[2])
    finish(ORDER[2])
    hidden(ORDER[3])
    graph_send(0, ORDER[2])
    down_wait(ORDER[3])
    finish(ORDER[3])

    def pairs(i, carry):
        a, b = in_ids[2 * i], in_ids[2 * i + 1]
        idr[pl.ds(i, 1), :] = jnp.where(low_lanes(a.shape), a, pltpu.roll(b, Q, 1))
        return carry

    lax.fori_loop(0, NG // 2, pairs, 0)
    graph_send(0, ORDER[3])

    def hot_rows(slot, p, row):
        col = column(row)
        for k in range(n_atoms // 128):
            lane = lax.broadcasted_iota(jnp.int32, (128, 128), 1).astype(F32) + 128.0 * k
            at[slot, 128 * (k // 8) : 128 * (k // 8) + 128, 128 * (k % 8) : 128 * (k % 8) + 128] = (
                jnp.where(col == lane, 1.0, 0.0).astype(BF)
            )

    def hot_targets(k):
        def body(i, carry):
            p = to_pair(k, i)
            hot_rows(4 * k + i, p, idr[pl.ds(p, 1), :])
            return carry

        lax.fori_loop(0, 4, body, 0)

    def hot_sources(k):
        def body(i, carry):
            p = from_pair(k, i)
            hot_rows(16 + 4 * k + i, p, pair_row(source, 2 * p, m) & 2047)
            return carry

        lax.fori_loop(0, 4, body, 0)

    def chunk_dot(th, k):
        base = th * h2
        for i in range(4):
            ids = lax.broadcasted_iota(jnp.int32, (h2, 128), 0) + base
            hot[:, 128 * i : 128 * (i + 1)] = jnp.where(
                idr[pl.ds(from_pair(k, i), 1), :] == ids, 1.0, 0.0
            ).astype(BF)
        rows = jnp.concatenate(
            [incoming[two(from_pair(k, i))].reshape(128, D) for i in range(4)], axis=0
        )
        return dot(hot[...], rows)

    load(3).wait()

    def seed(th, carry):
        pacc[th] = jnp.zeros((h2, D), F32)
        pacc[th, :, lanes_at(m, W)] = af_v[rows_at(th, h2), :].astype(F32)
        return carry

    lax.fori_loop(0, 2 * MP, seed, 0)
    for k in ORDER[:3]:
        graph_wait(0, k)

        def gather(th, carry, k=k):
            pacc[th] = pacc[th] + chunk_dot(th, k)
            return carry

        lax.fori_loop(0, 2 * MP, gather, 0)
    graph_wait(0, ORDER[3])

    def part(t, h):
        th = 2 * t + h
        return pacc[th] + chunk_dot(th, ORDER[3])

    def p_copy(n):
        t = (up, dn, up, dn, up, dn)[n]
        return remote(pbuf.at[n], rbuf.at[n], ps.at[n], pr.at[n], (g, t))

    pbuf[0] = part(op, 0).astype(BF)
    pbuf[1] = part(op, 1).astype(BF)
    p_copy(0).start()
    part_f[0] = part(up, 0)
    p_copy(1).start()
    part_f[1] = part(dn, 1)
    pbuf[2] = part(up, 1).astype(BF)
    pbuf[3] = part(dn, 0).astype(BF)
    p_copy(2).start()
    own[:h2, :] = part(m, 0)
    p_copy(3).start()
    own[h2:, :] = part(m, 1)
    for n in (1, 2):
        for k in range(1, NG):
            w_spread(n, k).start()
    p_copy(0).wait_recv()
    pbuf[4] = (part_f[0] + rbuf[0].astype(F32)).astype(BF)
    p_copy(1).wait_recv()
    pbuf[5] = (part_f[1] + rbuf[1].astype(F32)).astype(BF)
    p_copy(4).start()
    p_copy(5).start()
    for k in ORDER:
        hot_targets(k)
    w_spread_wait(1)
    for k in ORDER:
        graph_sent(0, k)

    def rows_of(src, h):
        return afull.at[pl.ds(pl.multiple_of(src * quarter + h * h2, h2), h2)]

    def own_copy(h, to):
        t = up if to == 0 else dn
        return remote(rows_of(m, h), rows_of(m, h), us.at[to, h], ur.at[to, h], (g, t))

    def relay(to):
        src, t = (dn, up) if to == 0 else (up, dn)
        return remote(rows_of(src, to), rows_of(src, to), us.at[2, to], ur.at[2, to], (g, t))

    for h in range(2):
        rows = slice(h * h2, (h + 1) * h2)
        a, b = ((3, 4), (2, 5))[h]
        p_copy(a).wait_recv()
        p_copy(b).wait_recv()
        mid = (own[rows, :] + rbuf[a].astype(F32) + rbuf[b].astype(F32)).astype(BF)
        new = (mid.astype(F32) + silu(dot(mid, w_full(1)))).astype(BF)
        afull[pl.ds(pl.multiple_of(m * quarter + h * h2, h2), h2), :] = new
        for to in (h, 1 - h):
            own_copy(h, to).start()
    hot_sources(ORDER[0])
    own_copy(0, 0).wait_recv()
    relay(0).start()
    own_copy(1, 1).wait_recv()
    relay(1).start()
    for k in ORDER[1:]:
        hot_sources(k)
    w_spread_wait(2)
    own_copy(0, 1).wait_recv()
    own_copy(1, 0).wait_recv()

    def pick(slot):
        n2 = n_atoms // 2
        hots = at[slot : slot + 4]
        return (
            dot(hots[:, :128].reshape(512, n2), afull[:n2, :])
            + dot(hots[:, 128:].reshape(512, n2), afull[n2:, :])
        ).astype(BF)

    def pick_from(slot, t):
        hots = at[slot : slot + 4, pl.ds(pl.multiple_of((t // 2) * 128, 128), 128), lanes_at(t % 2, 512)]
        return dot(hots.reshape(512, quarter), afull[rows_at(t, quarter), :])

    for k in ORDER:
        v = (pick_from(4 * k, m) + pick_from(4 * k, up) + pick_from(4 * k, dn)).astype(BF)
        v = v.reshape(4, 2, Q, D)
        for i in range(4):
            outg[two(to_pair(k, i))] = v[i]
    relay(0).wait_recv()
    relay(1).wait_recv()
    for n, k in enumerate(ORDER):
        v = pick_from(4 * k, op).astype(BF).reshape(4, 2, Q, D)
        for i in range(4):
            p = two(to_pair(k, i))
            outg[p] = outg[p] + v[i]
        if 0 < n < 3:
            graph_send(1, ORDER[n - 1])
    srcb[...] = pick(16 + 4 * ORDER[0]).reshape(4, 128, D)
    graph_sent(1, ORDER[0])
    graph_send(1, ORDER[2])

    def back(k, i, j):
        p, n = from_pair(k, i), 4 * k + i
        t = (m + j) % MP
        return remote(x.at[t, two(p)], out.at[two(p), m], zs.at[n, j], zr.at[n, j], (g, t))

    def here(k, i):
        p = from_pair(k, i)
        return pltpu.make_async_copy(x.at[m, two(p)], out.at[two(p), m], zl.at[4 * k + i])

    for n, k in enumerate(ORDER):
        if n > 0:
            srcb[...] = pick(16 + 4 * k).reshape(4, 128, D)
        if n == 1:
            aout[...] = afull[:, lanes_at(m, W)]
        def body(i, carry, k=k):
            p = from_pair(k, i)
            for s in (2 * p, 2 * p + 1):
                remote(outg.at[s], tbuf.at[s], xs.at[1, 0], xr.at[1, s], (s, m)).wait_recv()
            return edge_rows(k, i, carry)

        def edge_rows(k, i, carry):
            p = from_pair(k, i)
            pair = (srcb[i].astype(F32) * tbuf[two(p)].reshape(128, D).astype(F32)).astype(BF)
            v = (total[rows_at(p, 128), :] + silu(dot(pair, w_full(2)))).astype(BF)
            for j in range(MP):
                x[j, two(p)] = v[:, W * j : W * (j + 1)].reshape(2, Q, W)
            here(k, i).start()
            for j in (2, 1, 3):
                back(k, i, j).start()
            return carry

        if k == 0:
            graph_here(1).wait()
            s = g + 1 - 2 * core
            remote(outg.at[s], tbuf.at[s], xs.at[1, 0], xr.at[1, s], (s, m)).wait_recv()
            edge_rows(0, 0, 0)
            lax.fori_loop(1, 4, body, 0)
        else:
            lax.fori_loop(0, 4, body, 0)
        if n == 0:
            graph_sent(1, ORDER[1])
            graph_send(1, ORDER[3])
    for k in ORDER:
        for i in range(4):
            here(k, i).wait()
            for j in (2, 1, 3):
                back(k, i, j).wait()
                ef_copy(k, i, j).wait_send()
                down_copy(k, i, j).wait_send()
    for n in range(4):
        for j in (2, 1, 3):
            w_copy(n, j).wait_send()
    for n in range(3):
        for k in range(1, NG):
            w_spread(n, k).wait_send()
    for k in ORDER:
        graph_sent(2, k)
    for k in ORDER[2:]:
        graph_sent(1, k)
    for n in range(6):
        p_copy(n).wait_send()
    for h in range(2):
        for to in range(2):
            own_copy(h, to).wait_send()
        relay(h).wait_send()


def vmem(shape, dtype):
    return pltpu.VMEM(shape, dtype)


def local(
    edge_feats,
    edge_source,
    edge_target,
    edge_live,
    trip_partner,
    trip_mask,
    trip_basis,
    atom_feats,
    w_msg,
    w_down,
    w_bil,
    w_up,
    w_atom,
    w_edge,
):
    n_edges = edge_feats.shape[0]
    n_atoms = atom_feats.shape[0]
    rows = n_edges // MP
    quarter = n_atoms // MP
    half = quarter // 2
    dma = pltpu.SemaphoreType.DMA
    args = (
        edge_feats.reshape(NG, MP, Q, W),
        edge_target.reshape(2 * NG, 128),
        edge_live.reshape(2 * NG, 128),
        edge_source.reshape(2 * NG, 128),
        trip_partner,
        trip_mask,
        trip_basis.reshape(NG, MP, Q, 128),
        w_msg,
        jnp.transpose(w_down),
        jnp.transpose(w_bil),
        w_up,
        w_atom,
        w_edge,
        atom_feats,
    )
    spec = pl.BlockSpec(memory_space=pltpu.VMEM)
    hbm = pl.BlockSpec(memory_space=pl.ANY)
    edge_out, aout = pl.pallas_call(
        block_kernel,
        out_shape=(
            jax.ShapeDtypeStruct((NG, MP, Q, W), BF),
            jax.ShapeDtypeStruct((n_atoms, W), BF),
        ),
        in_specs=[hbm, spec, spec, spec, hbm, hbm, hbm, hbm, spec, spec, hbm, hbm, hbm, hbm],
        out_specs=(hbm, spec),
        scratch_shapes=[
            vmem((MP, NG, Q, W), BF),
            vmem((NG // 2, CAP, 128), BF),
            vmem((NG, CAP, NB * Q), BF),
            vmem((64, 16, 128), BF),
            vmem((SLOTS, 16, 128), BF),
            vmem((8 * DT, 1024), BF),
            vmem((128, 8 * DT), BF),
            vmem((rows, D), F32),
            vmem((NG, Q, D), BF),
            vmem((NG, Q, D), BF),
            vmem((NG, Q, D), BF),
            vmem((NG, 1, 128), jnp.int32),
            vmem((NG, 1, 128), jnp.int32),
            vmem((NG // 2, 128), jnp.int32),
            vmem((3, MP, D, W), BF),
            vmem((MP, DT, W), BF),
            vmem((half, 512), BF),
            vmem((2 * MP, half, D), F32),
            vmem((2, half, D), F32),
            vmem((quarter, D), F32),
            vmem((6, half, D), BF),
            vmem((6, half, D), BF),
            vmem((n_atoms, D), BF),
            vmem((4, 128, D), BF),
            vmem((NG, Q, 128), BF),
            vmem((SLOTS, n_edges), jnp.int32),
            vmem((SLOTS, n_edges), jnp.int32),
            vmem((n_atoms, W), BF),
            dma((4,)),
            dma((16, 4)),
            dma((16, 4)),
            dma((16,)),
            dma((16, 4)),
            dma((16, 4)),
            dma((4, 4)),
            dma((4, 4)),
            dma((4,)),
            dma((3, NG)),
            dma((3, NG)),
            dma((3, NG)),
            dma((3, NG)),
            dma((3,)),
            dma((6,)),
            dma((6,)),
            dma((3, 2)),
            dma((3, 2)),
            dma((16, 4)),
            dma((16, 4)),
            dma((16,)),
        ],
        compiler_params=pltpu.CompilerParams(
            collective_id=0, has_side_effects=True, vmem_limit_bytes=62 << 20
        ),
        name="block",
    )(*args)
    return (edge_out.reshape(n_edges, W), aout)


def solution(mesh):
    return jax.shard_map(
        local,
        mesh=mesh,
        in_specs=(
            P("graph", "mp"),
            P("graph"),
            P("graph"),
            P("graph"),
            P(None, "graph"),
            P(None, "graph"),
            P("graph", None),
            P("graph", "mp"),
            P(None, "mp"),
            P(),
            P(),
            P(None, "mp"),
            P(None, "mp"),
            P(None, "mp"),
        ),
        out_specs=(P("graph", "mp"), P("graph", "mp")),
        check_vma=False,
    )
```

```python
import jax
import jax.numpy as jnp
from jax import lax
from jax.experimental import pallas as pl
from jax.experimental.pallas import tpu as pltpu
from jax.sharding import PartitionSpec as P

DT = 64
NB = 16
SLOTS = 8
CAP = 256
MP = 4
Q = CAP // MP
NG = 32
BLK = 8
D = 512
W = D // MP
ORDER = (1, 3, 0, 2)
NEAR = (2, 1, 3, 0)
BF = jnp.bfloat16
F32 = jnp.float32
MESH = pl.DeviceIdType.MESH


def silu(v):
    h = 0.5 * v
    return h + h * jnp.tanh(h)


def dot(a, b):
    return jnp.dot(a, b, preferred_element_type=F32)


def lanes_at(k, n):
    return pl.ds(pl.multiple_of(k * n, n), n)


def rows_at(k, n):
    return pl.ds(pl.multiple_of(k * n, n), n)


def enter(g, m, over_graph):
    sem = pltpu.get_barrier_semaphore()
    peers = [(g, (m + k) % MP) for k in range(1, MP)]
    if over_graph:
        peers += [((g + k) % NG, m) for k in range(1, NG)]
    for peer in peers:
        pl.semaphore_signal(sem, inc=1, device_id=peer, device_id_type=MESH)
    pl.semaphore_wait(sem, len(peers))


def remote(src, dst, send, recv, peer):
    return pltpu.make_async_remote_copy(
        src_ref=src, dst_ref=dst, send_sem=send, recv_sem=recv, device_id=peer, device_id_type=MESH
    )


def low_lanes(shape):
    return lax.broadcasted_iota(jnp.int32, shape, len(shape) - 1) < Q


def pair_row(ref, blk, m):
    half = m // 2
    a = ref[pl.ds(2 * blk + half, 1), :]
    b = ref[pl.ds(2 * blk + 2 + half, 1), :]
    odd = m % 2 == 1
    ra, rb = pltpu.roll(a, Q, 1), pltpu.roll(b, Q, 1)
    return jnp.where(low_lanes(a.shape), jnp.where(odd, ra, a), jnp.where(odd, b, rb))


def column(row):
    return jnp.transpose(jnp.broadcast_to(row.astype(F32), (128, 128)))


def block_kernel(
    ef,
    target,
    live,
    source,
    partner,
    mask,
    basis,
    w_msg,
    w_down_t,
    w_bil_t,
    w_up,
    w_atom,
    w_edge,
    af,
    out,
    aout,
    x,
    dall,
    at,
    wrow,
    irow,
    mix,
    l_mat,
    total,
    outg,
    incoming,
    tbuf,
    idq,
    in_ids,
    idr,
    wf,
    up_f,
    hot,
    pacc,
    part_f,
    own,
    pbuf,
    rbuf,
    afull,
    srcb,
    basis_v,
    partner_v,
    mask_v,
    af_v,
    il,
    es,
    er,
    el,
    ds,
    dr,
    ws,
    wr,
    wl,
    vs,
    vr,
    xs,
    xr,
    xl,
    ps,
    pr,
    us,
    ur,
    zs,
    zr,
    zl,
):
    g = lax.axis_index("graph")
    m = lax.axis_index("mp")
    cx, cy, core = g // 8, (g // 2) % 4, g % 2
    quarter = own.shape[0]
    h2 = quarter // 2
    n_atoms = afull.shape[0]
    up, dn, op = (m + 1) % MP, (m + 3) % MP, (m + 2) % MP

    def to_pair(k, i):
        return ((cx + i) % 4) * 4 + (cy + k - i + 4) % 4

    def from_pair(k, i):
        return ((cx - i + 4) % 4) * 4 + (cy - k + i + 4) % 4

    def two(p):
        return pl.ds(2 * p, 2)

    loads = (
        (basis.at[:, m], basis_v),
        (partner, partner_v),
        (mask, mask_v),
        (af, af_v),
    )

    def load(n):
        return pltpu.make_async_copy(loads[n][0], loads[n][1], il.at[n])

    for n in range(4):
        load(n).start()
    enter(g, m, True)

    def ef_copy(k, i, j):
        p, n = to_pair(k, i), 4 * k + i
        t = (m + j) % MP
        return remote(ef.at[two(p), t], x.at[m, two(p)], es.at[n, j], er.at[n, j], (g, t))

    def ef_here(k, i):
        p = to_pair(k, i)
        return pltpu.make_async_copy(ef.at[two(p), m], x.at[m, two(p)], el.at[4 * k + i])

    def ef_start(k):
        for i in range(4):
            ef_here(k, i).start()
            for j in (2, 1, 3):
                ef_copy(k, i, j).start()

    def ef_wait(k):
        for i in range(4):
            ef_here(k, i).wait()
            for j in (2, 1, 3):
                ef_copy(k, i, j).wait_recv()

    def down_copy(k, i, j):
        p, n = to_pair(k, i), 4 * k + i
        d = dall.at[p, rows_at(m, Q), :]
        return remote(d, d, ds.at[n, j], dr.at[n, j], (g, (m + j) % MP))

    def down_start(k):
        for i in range(4):
            for j in (2, 1, 3):
                down_copy(k, i, j).start()

    def down_wait(k):
        for i in range(4):
            for j in (2, 1, 3):
                down_copy(k, i, j).wait_recv()

    weights = (w_msg, w_atom, w_edge)
    piece = pl.ds(pl.multiple_of(16 * g, 16), 16)

    def w_copy(n, j):
        peer = (g, (m + j) % MP)
        if n == 3:
            return remote(w_up, up_f.at[m], ws.at[n, j], wr.at[n, j], peer)
        return remote(weights[n].at[piece], wf.at[n, m, piece], ws.at[n, j], wr.at[n, j], peer)

    def w_here(n):
        if n == 3:
            return pltpu.make_async_copy(w_up, up_f.at[m], wl.at[n])
        return pltpu.make_async_copy(weights[n].at[piece], wf.at[n, m, piece], wl.at[n])

    def w_spread(n, k):
        d = (g + k) % NG
        ref = wf.at[n, :, piece]
        return remote(ref, ref, vs.at[n, k], vr.at[n, g], (d, m))

    def w_spread_wait(n):
        for k in range(1, NG):
            s = (g + k) % NG
            ref = wf.at[n, :, pl.ds(pl.multiple_of(16 * s, 16), 16)]
            remote(ref, ref, vs.at[n, k], vr.at[n, s], (s, m)).wait_recv()

    def w_full(n):
        return jnp.concatenate([wf[n, j] for j in range(MP)], axis=1)

    for n in range(4):
        w_here(n).start()
        for j in (2, 1, 3):
            w_copy(n, j).start()
    ef_start(ORDER[0])
    ef_start(ORDER[1])

    def write_ids(p, carry):
        row = pair_row(target, 2 * p, m) & 2047
        idq[2 * p] = row
        idq[2 * p + 1] = pltpu.roll(row, Q, 1)
        return carry

    lax.fori_loop(0, NG // 2, write_ids, 0)
    l_mat[:DT, :] = w_bil_t[:, : 8 * DT]
    l_mat[DT:, :] = w_bil_t[:, 8 * DT :]

    def weights_of(blk0):
        t = jnp.transpose(
            basis_v[pl.ds(blk0, 2)].reshape(128, 128).astype(F32)
        ).reshape(SLOTS, 2, 8, 128)
        lo, hi = t[:, 0], t[:, 1]
        low = low_lanes((SLOTS, 8, 128))
        return (
            jnp.where(low, lo, pltpu.roll(hi.reshape(64, 128), Q, 1).reshape(SLOTS, 8, 128)),
            jnp.where(low, pltpu.roll(lo.reshape(64, 128), Q, 1).reshape(SLOTS, 8, 128), hi),
        )

    def ids_of(blk):
        cols = lanes_at(2 * blk + m // 2, 128)
        v = jnp.where(mask_v[:, cols] != 0, partner_v[:, cols] & 255, -1)
        r = pltpu.roll(v, Q, 1)
        odd = m % 2 == 1
        low = low_lanes(v.shape)
        return jnp.where(low, jnp.where(odd, r, v), jnp.where(odd, v, r))

    def spread(k):
        one, zero = jnp.ones((2, 16, 128), BF), jnp.zeros((2, 16, 128), BF)

        def body(i, carry):
            blk0 = 2 * to_pair(k, i)
            both = weights_of(blk0)
            for half in range(2):
                blk = blk0 + half
                w = both[half]
                for s in range(SLOTS):
                    for j in range(8):
                        wrow[s * 8 + j] = jnp.broadcast_to(w[s, j : j + 1, :], (16, 128)).astype(BF)
                ids = ids_of(blk).astype(F32)
                for s in range(SLOTS):
                    irow[s] = jnp.broadcast_to(ids[s : s + 1, :], (16, 128)).astype(BF)

                def part(pt, carry):
                    p_ids = (
                        (lax.broadcasted_iota(jnp.int32, (32, 128), 0) + 32 * pt)
                        .astype(F32)
                        .astype(BF)
                        .reshape(2, 16, 128)
                    )
                    acc = [None] * 8
                    for s in range(SLOTS):
                        same = jnp.where(irow[s][None] == p_ids, one, zero)
                        for j in range(8):
                            term = same * wrow[s * 8 + j][None]
                            acc[j] = term if s == 0 else acc[j] + term
                    for j in range(8):
                        at[blk, rows_at(pt, 32), 128 * j : 128 * (j + 1)] = acc[j].reshape(32, 128)
                    return carry

                lax.fori_loop(0, 8, part, 0)
            return carry

        lax.fori_loop(0, 4, body, 0)

    def rows_of_x(p):
        return jnp.concatenate([x[j, two(p)].reshape(128, W) for j in range(MP)], axis=1)

    def down(k):
        def body(i, carry):
            p = to_pair(k, i)
            d = lax.dot_general(
                rows_of_x(p), w_down_t[...], (((1,), (1,)), ((), ())), preferred_element_type=F32
            )
            dall[p, rows_at(m, Q), :] = jnp.concatenate([d[:Q], d[Q:]], axis=1).astype(BF)
            return carry

        lax.fori_loop(0, 4, body, 0)

    def hidden(k):
        def body(i, carry):
            p = to_pair(k, i)
            rows = rows_of_x(p)
            total[rows_at(p, 128), :] = rows.astype(F32) + silu(dot(rows, w_full(0)))
            return carry

        lax.fori_loop(0, 4, body, 0)

    def finish(k):
        for i in range(4):
            p = to_pair(k, i)
            dt = jnp.transpose(dall[p].astype(F32)).astype(BF)
            for half in range(2):
                mixed = dot(dt[half * DT : (half + 1) * DT], at[2 * p + half]).astype(BF)
                mix[:, 256 * i + 128 * half : 256 * i + 128 * (half + 1)] = jnp.concatenate(
                    [mixed[:, 128 * j : 128 * (j + 1)] for j in range(8)], axis=0
                )
        o = dot(l_mat[...], mix[...])
        low = low_lanes((DT, 128))
        parts = []
        for i in range(4):
            a, b = o[:, 256 * i : 256 * i + 128], o[:, 256 * i + 128 : 256 * (i + 1)]
            parts.append(
                jnp.where(low, a[:DT] + pltpu.roll(a[DT:], Q, 1), pltpu.roll(b[:DT], Q, 1) + b[DT:])
            )
        up_all = jnp.concatenate([up_f[j] for j in range(MP)], axis=1)
        bil = jnp.transpose(jnp.concatenate(parts, axis=1)).astype(BF)
        for i in range(4):
            p = to_pair(k, i)
            rows = rows_at(p, 128)
            tot = total[rows, :] + dot(bil[128 * i : 128 * (i + 1)], up_all)
            total[rows, :] = tot
            alive = column(pair_row(live, 2 * p, m))
            alive = jnp.concatenate([alive] * 4, axis=1)
            outg[two(p)] = (tot * alive).astype(BF).reshape(2, Q, D)

    def targets(k):
        found = []
        for i in NEAR:
            n = 2 * (4 * k + i)
            p = to_pair(k, i)
            if k == 0 and i == 0:
                found.append((n, 2 * p + 1 - core))
            else:
                found += [(n, 2 * p), (n + 1, 2 * p + 1)]
        return found

    def sources(k):
        found = []
        for i in NEAR:
            p = from_pair(k, i)
            if k == 0 and i == 0:
                found.append(2 * p + 1 - core)
            else:
                found += [2 * p, 2 * p + 1]
        return found

    def graph_copy(q, n, d):
        src, dst = ((outg, incoming), (outg, tbuf), (idq, in_ids))[q]
        return remote(src.at[d], dst.at[g], xs.at[q, n], xr.at[q, g], (d, m))

    def graph_here(q):
        src, dst = ((outg, incoming), (outg, tbuf), (idq, in_ids))[q]
        return pltpu.make_async_copy(src.at[g], dst.at[g], xl.at[q])

    def graph_send(q, k):
        if k == 0:
            graph_here(q).start()
        for n, d in targets(k):
            graph_copy(q, n, d).start()

    def graph_wait(q, k):
        src, dst = ((outg, incoming), (outg, tbuf), (idq, in_ids))[q]
        if k == 0:
            graph_here(q).wait()
        for s in sources(k):
            remote(src.at[s], dst.at[s], xs.at[q, 0], xr.at[q, s], (s, m)).wait_recv()

    def graph_sent(q, k):
        for n, d in targets(k):
            graph_copy(q, n, d).wait_send()

    for n in range(3):
        load(n).wait()
    spread(ORDER[0])
    for n in range(4):
        w_here(n).wait()
        for j in (2, 1, 3):
            w_copy(n, j).wait_recv()
    for k in range(1, NG):
        w_spread(0, k).start()
    for k in ORDER:
        graph_send(2, k)
    ef_wait(ORDER[0])
    down(ORDER[0])
    down_start(ORDER[0])
    ef_start(ORDER[2])
    spread(ORDER[1])
    w_spread_wait(0)
    hidden(ORDER[0])
    ef_wait(ORDER[1])
    down(ORDER[1])
    down_start(ORDER[1])
    ef_start(ORDER[3])
    down_wait(ORDER[0])
    finish(ORDER[0])
    graph_send(0, ORDER[0])
    hidden(ORDER[1])
    spread(ORDER[2])
    ef_wait(ORDER[2])
    down(ORDER[2])
    down_start(ORDER[2])
    down_wait(ORDER[1])
    finish(ORDER[1])
    graph_send(0, ORDER[1])
    hidden(ORDER[2])
    spread(ORDER[3])
    ef_wait(ORDER[3])
    down(ORDER[3])
    down_start(ORDER[3])
    for k in ORDER:
        graph_wait(2, k)
    down_wait(ORDER[2])
    finish(ORDER[2])
    graph_send(0, ORDER[2])
    hidden(ORDER[3])
    down_wait(ORDER[3])
    finish(ORDER[3])

    def pairs(i, carry):
        a, b = in_ids[2 * i], in_ids[2 * i + 1]
        idr[pl.ds(i, 1), :] = jnp.where(low_lanes(a.shape), a, pltpu.roll(b, Q, 1))
        return carry

    lax.fori_loop(0, NG // 2, pairs, 0)
    graph_send(0, ORDER[3])

    def hot_rows(slot, p, row):
        col = column(row)
        for k in range(n_atoms // 128):
            lane = lax.broadcasted_iota(jnp.int32, (128, 128), 1).astype(F32) + 128.0 * k
            at[slot, 128 * (k // 8) : 128 * (k // 8) + 128, 128 * (k % 8) : 128 * (k % 8) + 128] = (
                jnp.where(col == lane, 1.0, 0.0).astype(BF)
            )

    def hot_targets(k):
        def body(i, carry):
            p = to_pair(k, i)
            hot_rows(4 * k + i, p, idr[pl.ds(p, 1), :])
            return carry

        lax.fori_loop(0, 4, body, 0)

    def hot_sources(k):
        def body(i, carry):
            p = from_pair(k, i)
            hot_rows(16 + 4 * k + i, p, pair_row(source, 2 * p, m) & 2047)
            return carry

        lax.fori_loop(0, 4, body, 0)

    def chunk_dot(th, k):
        base = th * h2
        for i in range(4):
            ids = lax.broadcasted_iota(jnp.int32, (h2, 128), 0) + base
            hot[:, 128 * i : 128 * (i + 1)] = jnp.where(
                idr[pl.ds(from_pair(k, i), 1), :] == ids, 1.0, 0.0
            ).astype(BF)
        rows = jnp.concatenate(
            [incoming[two(from_pair(k, i))].reshape(128, D) for i in range(4)], axis=0
        )
        return dot(hot[...], rows)

    load(3).wait()

    def seed(th, carry):
        pacc[th] = jnp.zeros((h2, D), F32)
        pacc[th, :, lanes_at(m, W)] = af_v[rows_at(th, h2), :].astype(F32)
        return carry

    lax.fori_loop(0, 2 * MP, seed, 0)
    for k in ORDER[:3]:
        graph_wait(0, k)

        def gather(th, carry, k=k):
            pacc[th] = pacc[th] + chunk_dot(th, k)
            return carry

        lax.fori_loop(0, 2 * MP, gather, 0)
    graph_wait(0, ORDER[3])

    def part(t, h):
        th = 2 * t + h
        return pacc[th] + chunk_dot(th, ORDER[3])

    def p_copy(n):
        t = (up, dn, up, dn, up, dn)[n]
        return remote(pbuf.at[n], rbuf.at[n], ps.at[n], pr.at[n], (g, t))

    pbuf[0] = part(op, 0).astype(BF)
    pbuf[1] = part(op, 1).astype(BF)
    p_copy(0).start()
    part_f[0] = part(up, 0)
    p_copy(1).start()
    part_f[1] = part(dn, 1)
    pbuf[2] = part(up, 1).astype(BF)
    pbuf[3] = part(dn, 0).astype(BF)
    p_copy(2).start()
    own[:h2, :] = part(m, 0)
    p_copy(3).start()
    own[h2:, :] = part(m, 1)
    for n in (1, 2):
        for k in range(1, NG):
            w_spread(n, k).start()
    p_copy(0).wait_recv()
    pbuf[4] = (part_f[0] + rbuf[0].astype(F32)).astype(BF)
    p_copy(1).wait_recv()
    pbuf[5] = (part_f[1] + rbuf[1].astype(F32)).astype(BF)
    p_copy(4).start()
    p_copy(5).start()
    for k in ORDER:
        hot_targets(k)
    w_spread_wait(1)
    for k in ORDER:
        graph_sent(0, k)

    def rows_of(src, h):
        return afull.at[pl.ds(pl.multiple_of(src * quarter + h * h2, h2), h2)]

    def own_copy(h, to):
        t = up if to == 0 else dn
        return remote(rows_of(m, h), rows_of(m, h), us.at[to, h], ur.at[to, h], (g, t))

    def relay(to):
        src, t = (dn, up) if to == 0 else (up, dn)
        return remote(rows_of(src, to), rows_of(src, to), us.at[2, to], ur.at[2, to], (g, t))

    for h in range(2):
        rows = slice(h * h2, (h + 1) * h2)
        a, b = ((3, 4), (2, 5))[h]
        p_copy(a).wait_recv()
        p_copy(b).wait_recv()
        mid = (own[rows, :] + rbuf[a].astype(F32) + rbuf[b].astype(F32)).astype(BF)
        new = (mid.astype(F32) + silu(dot(mid, w_full(1)))).astype(BF)
        afull[pl.ds(pl.multiple_of(m * quarter + h * h2, h2), h2), :] = new
        for to in (h, 1 - h):
            own_copy(h, to).start()
    hot_sources(ORDER[0])
    own_copy(0, 0).wait_recv()
    relay(0).start()
    own_copy(1, 1).wait_recv()
    relay(1).start()
    for k in ORDER[1:]:
        hot_sources(k)
    w_spread_wait(2)
    own_copy(0, 1).wait_recv()
    own_copy(1, 0).wait_recv()

    def pick(slot):
        n2 = n_atoms // 2
        hots = at[slot : slot + 4]
        return (
            dot(hots[:, :128].reshape(512, n2), afull[:n2, :])
            + dot(hots[:, 128:].reshape(512, n2), afull[n2:, :])
        ).astype(BF)

    def pick_from(slot, t):
        hots = at[slot : slot + 4, pl.ds(pl.multiple_of((t // 2) * 128, 128), 128), lanes_at(t % 2, 512)]
        return dot(hots.reshape(512, quarter), afull[rows_at(t, quarter), :])

    for k in ORDER:
        v = (pick_from(4 * k, m) + pick_from(4 * k, up) + pick_from(4 * k, dn)).astype(BF)
        v = v.reshape(4, 2, Q, D)
        for i in range(4):
            outg[two(to_pair(k, i))] = v[i]
    relay(0).wait_recv()
    relay(1).wait_recv()
    for n, k in enumerate(ORDER):
        v = pick_from(4 * k, op).astype(BF).reshape(4, 2, Q, D)
        for i in range(4):
            p = two(to_pair(k, i))
            outg[p] = outg[p] + v[i]
        if 0 < n < 3:
            graph_send(1, ORDER[n - 1])
    srcb[...] = pick(16 + 4 * ORDER[0]).reshape(4, 128, D)
    graph_sent(1, ORDER[0])
    graph_send(1, ORDER[2])

    def back(k, i, j):
        p, n = from_pair(k, i), 4 * k + i
        t = (m + j) % MP
        return remote(x.at[t, two(p)], out.at[two(p), m], zs.at[n, j], zr.at[n, j], (g, t))

    def here(k, i):
        p = from_pair(k, i)
        return pltpu.make_async_copy(x.at[m, two(p)], out.at[two(p), m], zl.at[4 * k + i])

    for n, k in enumerate(ORDER):
        if n > 0:
            srcb[...] = pick(16 + 4 * k).reshape(4, 128, D)
        if n == 1:
            aout[...] = afull[:, lanes_at(m, W)]
        def body(i, carry, k=k):
            p = from_pair(k, i)
            for s in (2 * p, 2 * p + 1):
                remote(outg.at[s], tbuf.at[s], xs.at[1, 0], xr.at[1, s], (s, m)).wait_recv()
            return edge_rows(k, i, carry)

        def edge_rows(k, i, carry):
            p = from_pair(k, i)
            pair = (srcb[i].astype(F32) * tbuf[two(p)].reshape(128, D).astype(F32)).astype(BF)
            v = (total[rows_at(p, 128), :] + silu(dot(pair, w_full(2)))).astype(BF)
            for j in range(MP):
                x[j, two(p)] = v[:, W * j : W * (j + 1)].reshape(2, Q, W)
            here(k, i).start()
            for j in (2, 1, 3):
                back(k, i, j).start()
            return carry

        if k == 0:
            graph_here(1).wait()
            s = g + 1 - 2 * core
            remote(outg.at[s], tbuf.at[s], xs.at[1, 0], xr.at[1, s], (s, m)).wait_recv()
            edge_rows(0, 0, 0)
            lax.fori_loop(1, 4, body, 0)
        else:
            lax.fori_loop(0, 4, body, 0)
        if n == 0:
            graph_sent(1, ORDER[1])
            graph_send(1, ORDER[3])
    for k in ORDER:
        for i in range(4):
            here(k, i).wait()
            for j in (2, 1, 3):
                back(k, i, j).wait()
                ef_copy(k, i, j).wait_send()
                down_copy(k, i, j).wait_send()
    for n in range(4):
        for j in (2, 1, 3):
            w_copy(n, j).wait_send()
    for n in range(3):
        for k in range(1, NG):
            w_spread(n, k).wait_send()
    for k in ORDER:
        graph_sent(2, k)
    for k in ORDER[2:]:
        graph_sent(1, k)
    for n in range(6):
        p_copy(n).wait_send()
    for h in range(2):
        for to in range(2):
            own_copy(h, to).wait_send()
        relay(h).wait_send()


def vmem(shape, dtype):
    return pltpu.VMEM(shape, dtype)


def local(
    edge_feats,
    edge_source,
    edge_target,
    edge_live,
    trip_partner,
    trip_mask,
    trip_basis,
    atom_feats,
    w_msg,
    w_down,
    w_bil,
    w_up,
    w_atom,
    w_edge,
):
    n_edges = edge_feats.shape[0]
    n_atoms = atom_feats.shape[0]
    rows = n_edges // MP
    quarter = n_atoms // MP
    half = quarter // 2
    dma = pltpu.SemaphoreType.DMA
    args = (
        edge_feats.reshape(NG, MP, Q, W),
        edge_target.reshape(2 * NG, 128),
        edge_live.reshape(2 * NG, 128),
        edge_source.reshape(2 * NG, 128),
        trip_partner,
        trip_mask,
        trip_basis.reshape(NG, MP, Q, 128),
        w_msg,
        jnp.transpose(w_down),
        jnp.transpose(w_bil),
        w_up,
        w_atom,
        w_edge,
        atom_feats,
    )
    spec = pl.BlockSpec(memory_space=pltpu.VMEM)
    hbm = pl.BlockSpec(memory_space=pl.ANY)
    edge_out, aout = pl.pallas_call(
        block_kernel,
        out_shape=(
            jax.ShapeDtypeStruct((NG, MP, Q, W), BF),
            jax.ShapeDtypeStruct((n_atoms, W), BF),
        ),
        in_specs=[hbm, spec, spec, spec, hbm, hbm, hbm, hbm, spec, spec, hbm, hbm, hbm, hbm],
        out_specs=(hbm, spec),
        scratch_shapes=[
            vmem((MP, NG, Q, W), BF),
            vmem((NG // 2, CAP, 128), BF),
            vmem((NG, CAP, NB * Q), BF),
            vmem((64, 16, 128), BF),
            vmem((SLOTS, 16, 128), BF),
            vmem((8 * DT, 1024), BF),
            vmem((128, 8 * DT), BF),
            vmem((rows, D), F32),
            vmem((NG, Q, D), BF),
            vmem((NG, Q, D), BF),
            vmem((NG, Q, D), BF),
            vmem((NG, 1, 128), jnp.int32),
            vmem((NG, 1, 128), jnp.int32),
            vmem((NG // 2, 128), jnp.int32),
            vmem((3, MP, D, W), BF),
            vmem((MP, DT, W), BF),
            vmem((half, 512), BF),
            vmem((2 * MP, half, D), F32),
            vmem((2, half, D), F32),
            vmem((quarter, D), F32),
            vmem((6, half, D), BF),
            vmem((6, half, D), BF),
            vmem((n_atoms, D), BF),
            vmem((4, 128, D), BF),
            vmem((NG, Q, 128), BF),
            vmem((SLOTS, n_edges), jnp.int32),
            vmem((SLOTS, n_edges), jnp.int32),
            vmem((n_atoms, W), BF),
            dma((4,)),
            dma((16, 4)),
            dma((16, 4)),
            dma((16,)),
            dma((16, 4)),
            dma((16, 4)),
            dma((4, 4)),
            dma((4, 4)),
            dma((4,)),
            dma((3, NG)),
            dma((3, NG)),
            dma((3, NG)),
            dma((3, NG)),
            dma((3,)),
            dma((6,)),
            dma((6,)),
            dma((3, 2)),
            dma((3, 2)),
            dma((16, 4)),
            dma((16, 4)),
            dma((16,)),
        ],
        compiler_params=pltpu.CompilerParams(
            collective_id=0, has_side_effects=True, vmem_limit_bytes=62 << 20
        ),
        name="block",
    )(*args)
    return (edge_out.reshape(n_edges, W), aout)


def solution(mesh):
    return jax.shard_map(
        local,
        mesh=mesh,
        in_specs=(
            P("graph", "mp"),
            P("graph"),
            P("graph"),
            P("graph"),
            P(None, "graph"),
            P(None, "graph"),
            P("graph", None),
            P("graph", "mp"),
            P(None, "mp"),
            P(),
            P(),
            P(None, "mp"),
            P(None, "mp"),
            P(None, "mp"),
        ),
        out_specs=(P("graph", "mp"), P("graph", "mp")),
        check_vma=False,
    )
```
